128 devices in a mesh: ctx: 32 (over z, x, core), head: 4 (over y).
Axes of the slice: x: 4, y: 4, z: 4, core: 2. Of those that a mesh axis runs over, the one named last changes fastest.
Arguments:
- queries: bfloat16 [32768, 2048], P('ctx', 'head'), may hold values from -8 to 8
- keys: bfloat16 [32768, 2048], P('ctx', 'head'), may hold values from -8 to 8
- values: bfloat16 [32768, 2048], P('ctx', 'head'), may hold values from -6 to 6
- out_weight: bfloat16 [4096, 2048], P(None, 'head'), may hold values from -0.125 to 0.125
- out_grad: bfloat16 [32768, 4096], P('ctx', 'head'), may hold values from -6 to 6
- long_blocks: int32 [64, 4], replicated, may hold values from 0 to 63, as said below
Outputs:
- layer_out: bfloat16 [32768, 4096], P('ctx', 'head')
- query_grad: bfloat16 [32768, 2048], P('ctx', 'head')
- key_grad: bfloat16 [32768, 2048], P('ctx', 'head')
- value_grad: bfloat16 [32768, 2048], P('ctx', 'head')
The draws below stay inside these ranges and needn't reach their ends.
Inputs may be any that keep to these rules, and one draw needn't show every extreme that they name: `long_blocks`: row b names 4 different blocks. The 8 blocks named by the rows of the 2 query blocks held by one index of ctx lie on 8 different indices of ctx. A row may name its own block.
All inputs are finite; a program needn't handle non-finite values.
Results may differ from the reference program's by a relative error of at most 0.019.
Values may be sent and summed in bfloat16 or wider, within the bound.
No kernel may reach another device: no remote copies, remote signals or barrier semaphores. Data moves between devices by JAX's collectives and lax.ppermute only.
A program may use at most 192 MiB of HBM per device.

```python
import math
import jax
import jax.numpy as jnp
from jax import lax

D = 4096
HD = 128
LIN_DEV = 3
LISTED = 4
BLOCK = 512
BLOCKS_DEV = 2
TOKENS = 32768
NBLK = 64
HEADS = 16
N_HEAD = 4


def base_draw(key):
    return jnp.clip(jax.random.normal(key, (TOKENS, HEADS * HD), jnp.float32), -6.0, 6.0)


def draw_queries(key, part):
    drawn = base_draw(jax.random.fold_in(key, 1))
    return drawn.astype(jnp.bfloat16)


def draw_keys(key, part):
    drawn = base_draw(jax.random.fold_in(key, 2))
    return drawn.astype(jnp.bfloat16)


def draw_long_blocks(key, part):
    devices = NBLK // BLOCKS_DEV
    requests = LISTED * BLOCKS_DEV
    key_order, key_score, key_offset = jax.random.split(jax.random.fold_in(key, 11), 3)
    shuffled = jax.random.permutation(key_order, devices)
    favored = jnp.where(shuffled < max(1, devices // 8), 4 * devices, 0)
    scores = jax.random.randint(key_score, (devices, devices), 0, 4 * devices) + favored[None, :]
    distinct = scores * devices + jnp.arange(devices)[None, :]
    ranked = jnp.argsort(-distinct, axis=1)
    request_ids = jnp.arange(requests)
    owners = ranked[:, request_ids % devices]
    offsets = jax.random.randint(key_offset, (devices, devices), 0, BLOCKS_DEV)
    picked = (jnp.take_along_axis(offsets, owners, axis=1) + request_ids[None, :] // devices) % BLOCKS_DEV
    return (owners * BLOCKS_DEV + picked).reshape(NBLK, LISTED).astype(jnp.int32)


def shard_levels(own_key, extent, cuts, smallest, top_value):
    def one(position, blocks):
        heights = jax.random.uniform(jax.random.fold_in(jax.random.fold_in(own_key, 6), position), (blocks,), jnp.float32, smallest / len(cuts), top_value / len(cuts))
        return jnp.repeat(jnp.exp(heights), extent[position] // blocks).reshape((-1,) + (1,) * (len(extent) - position - 1))

    factor_of = one(*cuts[0])
    for cut in cuts[1:]:
        factor_of = factor_of * one(*cut)
    return factor_of


def normal_values(own_key, dims, deviation, limit, cuts=(), kind=jnp.bfloat16):
    values = deviation * jax.random.normal(own_key, dims, jnp.float32)
    if cuts:
        values = values * shard_levels(own_key, dims, cuts, -0.22, 0.18)
    return jnp.clip(values, -limit, limit).astype(kind)


def setup_inputs(seed: int = 0) -> dict:
    streams_of = jax.random.split(jax.random.key(seed), 7)
    queries = draw_queries(jax.random.fold_in(streams_of[6], 71), 0)
    keys = draw_keys(jax.random.fold_in(streams_of[6], 71), 0)
    values = normal_values(streams_of[2], (TOKENS, HEADS * HD), 1.0, 6.0, ((0, 32), (1, 4)))
    out_weight = normal_values(streams_of[3], (D, HEADS * HD), (HEADS * HD) ** -0.5, 0.125, ((1, 4),))
    out_grad = normal_values(streams_of[4], (TOKENS, D), 1.0, 6.0, ((0, 32), (1, 4)))
    long_blocks = draw_long_blocks(jax.random.fold_in(streams_of[6], 71), 0)
    return {"queries": queries, "keys": keys, "values": values, "out_weight": out_weight, "out_grad": out_grad, "long_blocks": long_blocks}


highest = lax.Precision.HIGHEST

def split_heads(array):
    shaped = array.reshape(NBLK, BLOCK, N_HEAD, LIN_DEV + 1, HD)
    linear = shaped[:, :, :, :LIN_DEV].reshape(NBLK, BLOCK, N_HEAD * LIN_DEV, HD)
    sparse = shaped[:, :, :, LIN_DEV]
    return (linear, sparse)

def join_heads(linear, sparse):
    shaped = linear.reshape(NBLK, BLOCK, N_HEAD, LIN_DEV, HD)
    merged = jnp.concatenate([shaped, sparse[:, :, :, None]], axis=3)
    return merged.reshape(TOKENS, HEADS * HD)

def reference(queries, keys, values, out_weight, out_grad, long_blocks):
    causal = jnp.arange(BLOCK)[:, None] >= jnp.arange(BLOCK)[None, :]
    scaling = 1.0 / math.sqrt(HD)
    positions = jnp.arange(TOKENS, dtype=jnp.int32).reshape(NBLK, BLOCK)
    pos_scale = 1.0 / (math.sqrt(HD) * jnp.sqrt((positions + 1).astype(jnp.float32)))
    attn_grad = jnp.dot(out_grad, out_weight, preferred_element_type=jnp.float32).astype(jnp.bfloat16)
    lin_q, sparse_q = split_heads(queries)
    lin_k, sparse_k = split_heads(keys)
    lin_v, sparse_v = split_heads(values)
    lin_grad, sparse_grad = split_heads(attn_grad)

    def lin_scores_of(query_rows, key_rows, scale_row):
        scores = jnp.einsum('uhd,shd->hus', query_rows.astype(jnp.float32), key_rows.astype(jnp.float32))
        return jnp.where(causal[None], scale_row[None, :, None] * scores, 0.0).astype(jnp.bfloat16)

    def forward_step(state_now, block_in):
        query_rows, key_rows, value_rows, scale_row = block_in
        weights = lin_scores_of(query_rows, key_rows, scale_row)
        inside_block = jnp.einsum('hus,she->uhe', weights.astype(jnp.float32), value_rows.astype(jnp.float32))
        across = jnp.einsum('uhd,hde->uhe', query_rows.astype(jnp.float32), state_now, precision=highest)
        output = (inside_block + scale_row[:, None, None] * across).astype(jnp.bfloat16)
        state_next = state_now + jnp.einsum('shd,she->hde', key_rows.astype(jnp.float32), value_rows.astype(jnp.float32))
        return (state_next, (output, state_now))
    zero_state = jnp.zeros((N_HEAD * LIN_DEV, HD, HD), jnp.float32)
    final_state, (lin_out, state_before) = lax.scan(forward_step, zero_state, (lin_q, lin_k, lin_v, pos_scale))

    def backward_step(adj_after, block_in):
        query_rows, key_rows, value_rows, scale_row, grad_rows, state_now = block_in
        weights = lin_scores_of(query_rows, key_rows, scale_row)
        grad_scores = jnp.einsum('uhe,she->hus', grad_rows.astype(jnp.float32), value_rows.astype(jnp.float32))
        grad_weights = jnp.where(causal[None], scale_row[None, :, None] * grad_scores, 0.0).astype(jnp.bfloat16)
        scaled_grad = (scale_row[:, None, None] * grad_rows.astype(jnp.float32)).astype(jnp.bfloat16)
        grad_q = jnp.einsum('hus,shd->uhd', grad_weights.astype(jnp.float32), key_rows.astype(jnp.float32))
        grad_q = grad_q + scale_row[:, None, None] * jnp.einsum('uhe,hde->uhd', grad_rows.astype(jnp.float32), state_now, precision=highest)
        grad_k = jnp.einsum('hus,uhd->shd', grad_weights.astype(jnp.float32), query_rows.astype(jnp.float32))
        grad_k = grad_k + jnp.einsum('she,hde->shd', value_rows.astype(jnp.float32), adj_after, precision=highest)
        grad_v = jnp.einsum('hus,uhe->she', weights.astype(jnp.float32), grad_rows.astype(jnp.float32))
        grad_v = grad_v + jnp.einsum('shd,hde->she', key_rows.astype(jnp.float32), adj_after, precision=highest)
        adj_next = adj_after + jnp.einsum('uhd,uhe->hde', query_rows.astype(jnp.float32), scaled_grad.astype(jnp.float32))
        return (adj_next, (grad_q, grad_k, grad_v))
    total_adj, (lin_dq, lin_dk, lin_dv) = lax.scan(backward_step, zero_state, (lin_q, lin_k, lin_v, pos_scale, lin_grad, state_before), reverse=True)

    def sparse_step(block_in):
        query_rows, key_rows, value_rows, grad_rows, listed, index_here = block_in
        far_keys = jnp.take(sparse_k, listed, axis=0).astype(jnp.float32)
        far_values = jnp.take(sparse_v, listed, axis=0).astype(jnp.float32)
        usable = listed != index_here
        query_f = query_rows.astype(jnp.float32)
        key_f = key_rows.astype(jnp.float32)
        value_f = value_rows.astype(jnp.float32)
        grad_f = grad_rows.astype(jnp.float32)
        own_scores = scaling * jnp.einsum('uhd,shd->hus', query_f, key_f)
        own_scores = jnp.where(causal[None], own_scores, -jnp.inf)
        far_scores = scaling * jnp.einsum('uhd,rshd->hurs', query_f, far_keys)
        far_scores = jnp.where(usable[None, None, :, None], far_scores, -jnp.inf)
        row_peak = jnp.maximum(lax.optimization_barrier(jnp.max(own_scores, axis=2)), lax.optimization_barrier(jnp.max(far_scores, axis=(2, 3))))
        own_exp = jnp.exp(own_scores - row_peak[:, :, None])
        far_exp = jnp.exp(far_scores - row_peak[:, :, None, None])
        row_sums = lax.optimization_barrier(jnp.sum(own_exp, axis=2)) + lax.optimization_barrier(jnp.sum(far_exp, axis=(2, 3)))
        own_prob = own_exp / row_sums[:, :, None]
        far_prob = far_exp / row_sums[:, :, None, None]
        own_weight = own_prob.astype(jnp.bfloat16).astype(jnp.float32)
        far_weight = far_prob.astype(jnp.bfloat16).astype(jnp.float32)
        output = (jnp.einsum('hus,shd->uhd', own_weight, value_f) + jnp.einsum('hurs,rshd->uhd', far_weight, far_values)).astype(jnp.bfloat16)
        row_dot = lax.optimization_barrier(jnp.sum(grad_f * output.astype(jnp.float32), axis=-1)).T
        own_dp = jnp.einsum('uhd,shd->hus', grad_f, value_f)
        far_dp = jnp.einsum('uhd,rshd->hurs', grad_f, far_values)
        own_ds = (own_prob * (own_dp - row_dot[:, :, None])).astype(jnp.bfloat16).astype(jnp.float32)
        far_ds = (far_prob * (far_dp - row_dot[:, :, None, None])).astype(jnp.bfloat16).astype(jnp.float32)
        grad_q = scaling * (jnp.einsum('hus,shd->uhd', own_ds, key_f) + jnp.einsum('hurs,rshd->uhd', far_ds, far_keys))
        own_dk = scaling * jnp.einsum('hus,uhd->shd', own_ds, query_f)
        own_dv = jnp.einsum('hus,uhd->shd', own_weight, grad_f)
        pair_k = (scaling * jnp.einsum('hurs,uhd->rshd', far_ds, query_f)).astype(jnp.bfloat16)
        pair_v = jnp.einsum('hurs,uhd->rshd', far_weight, grad_f).astype(jnp.bfloat16)
        return (output, grad_q, own_dk, own_dv, pair_k, pair_v)
    block_ids = jnp.arange(NBLK, dtype=jnp.int32)
    sparse_out, sparse_dq, own_dk, own_dv, pair_k, pair_v = lax.map(sparse_step, (sparse_q, sparse_k, sparse_v, sparse_grad, long_blocks, block_ids))
    flat_ids = long_blocks.reshape(-1)
    far_dk = jax.ops.segment_sum(pair_k.reshape(NBLK * LISTED, BLOCK, N_HEAD, HD).astype(jnp.float32), flat_ids, num_segments=NBLK)
    far_dv = jax.ops.segment_sum(pair_v.reshape(NBLK * LISTED, BLOCK, N_HEAD, HD).astype(jnp.float32), flat_ids, num_segments=NBLK)
    sparse_dk = own_dk + far_dk
    sparse_dv = own_dv + far_dv
    attention = join_heads(lin_out, sparse_out)
    width = (LIN_DEV + 1) * HD
    layer_sum = jnp.zeros((TOKENS, D), jnp.float32)
    for group_id in range(N_HEAD):
        part_out = lax.dot_general(attention[:, group_id * width:(group_id + 1) * width], out_weight[:, group_id * width:(group_id + 1) * width], (((1,), (1,)), ((), ())), preferred_element_type=jnp.float32)
        rounded = lax.optimization_barrier(part_out.astype(jnp.bfloat16))
        layer_sum = layer_sum + rounded.astype(jnp.float32)
    layer_out = layer_sum.astype(jnp.bfloat16)
    query_grad = join_heads(lin_dq, sparse_dq).astype(jnp.bfloat16)
    key_grad = join_heads(lin_dk, sparse_dk).astype(jnp.bfloat16)
    value_grad = join_heads(lin_dv, sparse_dv).astype(jnp.bfloat16)
    return (layer_out, query_grad, key_grad, value_grad)
```

```python
import math

import jax
import jax.numpy as jnp
from jax import lax
from jax.experimental import pallas as pl
from jax.experimental.pallas import tpu as pltpu
from jax.sharding import PartitionSpec as P

HD = 128
LIN = 3
LISTED = 4
BLOCK = 512
SIDE = 4
CORES = 2
CTX = SIDE * SIDE * CORES
SCALING = 1.0 / math.sqrt(HD)
BF = jnp.bfloat16
F32 = jnp.float32
MIB = 1 << 20
TILE = (BLOCK, HD)


def dot(a, b, ca, cb):
    return lax.dot_general(a, b, (((ca,), (cb,)), ((), ())), preferred_element_type=F32)


def params(mib):
    return pltpu.CompilerParams(vmem_limit_bytes=mib * MIB)


def cost(flops, nbytes):
    return pl.CostEstimate(flops=int(flops), bytes_accessed=int(nbytes), transcendentals=0)


def shift(value, dz=0, dx=0, dc=0):
    pairs = []
    for z in range(SIDE):
        for x in range(SIDE):
            for c in range(CORES):
                to = (((z + dz) % SIDE) * SIDE + (x + dx) % SIDE) * CORES + (c + dc) % CORES
                pairs.append(((z * SIDE + x) * CORES + c, to))
    return lax.ppermute(value, "ctx", pairs)


def along(axis):
    def move(value, step):
        return shift(value, dz=step) if axis == "z" else shift(value, dx=step)

    return move


def swap(value):
    return shift(value, dc=1)


def ring_gather(value, axis):
    move = along(axis)
    half = value.shape[0] // 2
    right = move(value, 1)
    left = move(value, -1)
    far_a = move(right[:half], 1)
    far_b = move(left[half:], -1)
    return [value, right, far_a, far_b, left]


def scan_states(own, backward):
    total = jnp.zeros_like(own)
    step = 1
    while step < CTX:
        if backward:
            pairs = [(i + step, i) for i in range(CTX - step)]
        else:
            pairs = [(i, i + step) for i in range(CTX - step)]
        total = total + lax.ppermute((own + total).astype(BF), "ctx", pairs).astype(F32)
        step *= 2
    return total


def causal_mask():
    s = lax.broadcasted_iota(jnp.int32, (BLOCK, BLOCK), 0)
    u = lax.broadcasted_iota(jnp.int32, (BLOCK, BLOCK), 1)
    return s <= u


def states_kernel(k_ref, v_ref, out_ref):
    out_ref[0, 0] = dot(k_ref[...], v_ref[...], 0, 0)


def adjoint_kernel(q_ref, g_ref, c_ref, out_ref):
    qt = (q_ref[...].astype(F32).T * c_ref[0:1, :]).astype(BF)
    out_ref[0, 0] = dot(qt, g_ref[...], 1, 0)


def tile_spec():
    return pl.BlockSpec(TILE, lambda i, h: (i, h))


def scale_spec():
    return pl.BlockSpec((8, BLOCK), lambda i, h: (0, i))


def state_spec():
    return pl.BlockSpec((1, 1, HD, HD), lambda i, h: (i, h, 0, 0))


def block_states(keys, values):
    return pl.pallas_call(
        states_kernel,
        grid=(2, LIN),
        in_specs=[tile_spec(), tile_spec()],
        out_specs=state_spec(),
        out_shape=jax.ShapeDtypeStruct((2, LIN, HD, HD), F32),
        compiler_params=params(16),
        cost_estimate=cost(1e8, 2 * MIB),
        name="block_states",
    )(keys, values)


def block_adjoints(queries, grads, scale):
    return pl.pallas_call(
        adjoint_kernel,
        grid=(2, LIN),
        in_specs=[tile_spec(), tile_spec(), scale_spec()],
        out_specs=state_spec(),
        out_shape=jax.ShapeDtypeStruct((2, LIN, HD, HD), F32),
        compiler_params=params(16),
        cost_estimate=cost(1e8, 2 * MIB),
        name="block_adjoints",
    )(queries, grads, scale)


def linear_forward_kernel(q_ref, k_ref, v_ref, c_ref, hi_ref, lo_ref, out_ref):
    q, k, v, c = q_ref[...], k_ref[...], v_ref[...], c_ref[0:1, :]
    weights = jnp.where(causal_mask(), dot(k, q, 1, 1) * c, 0.0).astype(BF)
    out = dot(v, weights, 0, 0)
    out = out + c * (dot(hi_ref[0, 0], q, 1, 1) + dot(lo_ref[0, 0], q, 1, 1))
    out_ref[...] = out.T.astype(BF)


def linear_forward(queries, keys, values, scale, hi, lo):
    return pl.pallas_call(
        linear_forward_kernel,
        grid=(2, LIN),
        in_specs=[tile_spec()] * 3 + [scale_spec(), state_spec(), state_spec()],
        out_specs=tile_spec(),
        out_shape=jax.ShapeDtypeStruct(queries.shape, BF),
        compiler_params=params(24),
        cost_estimate=cost(2.4e9, 4 * MIB),
        name="linear_forward",
    )(queries, keys, values, scale, hi, lo)


def linear_backward_kernel(
    q_ref, k_ref, v_ref, g_ref, c_ref, sh_ref, sl_ref, ah_ref, al_ref, base_ref, dq_ref, dk_ref, dv_ref
):
    q, k, v, g, c = q_ref[...], k_ref[...], v_ref[...], g_ref[...], c_ref[0:1, :]
    mask = causal_mask()
    grad_weights = jnp.where(mask, dot(v, g, 1, 1) * c, 0.0).astype(BF)
    dq = dot(k, grad_weights, 0, 0)
    dq = dq + c * (dot(sh_ref[0, 0], g, 1, 1) + dot(sl_ref[0, 0], g, 1, 1))
    dq_ref[...] = dq.T.astype(BF)
    dk = dot(grad_weights, q, 1, 0) + dot(v, ah_ref[0, 0], 1, 1) + dot(v, al_ref[0, 0], 1, 1)
    dk_ref[...] = dk.astype(BF)
    weights = jnp.where(mask, dot(k, q, 1, 1) * c, 0.0).astype(BF)
    dv = dot(weights, g, 1, 0) + dot(k, ah_ref[0, 0], 1, 0) + dot(k, al_ref[0, 0], 1, 0)
    dv_ref[...] = dv.astype(BF)


def linear_backward(queries, keys, values, grads, scale, sh, sl, ah, al, base):
    shape = jax.ShapeDtypeStruct(queries.shape, BF)
    return pl.pallas_call(
        linear_backward_kernel,
        grid=(2, LIN),
        in_specs=[tile_spec()] * 4
        + [scale_spec()]
        + [state_spec()] * 4
        + [pl.BlockSpec(memory_space=pl.ANY)],
        out_specs=[tile_spec()] * 3,
        out_shape=[shape] * 3,
        input_output_aliases={9: 0},
        compiler_params=params(24),
        cost_estimate=cost(5e9, 8 * MIB),
        name="linear_backward",
    )(queries, keys, values, grads, scale, sh, sl, ah, al, base)


def sparse_forward_kernel(table, q_ref, k_ref, v_ref, base_ref, *rest):
    k_pieces, v_pieces = rest[:10], rest[10:20]
    out_ref, p_ref, kf_ref, vf_ref, s_ref, sems = rest[20:]
    step = pl.program_id(0)
    for r in range(LISTED):
        row = step * LISTED + r
        for j in range(10):

            @pl.when(table[row, 0] == j)
            def _():
                pltpu.make_async_copy(
                    k_pieces[j].at[table[row, 1]], kf_ref.at[r], sems.at[0, r]
                ).start()

            @pl.when(table[row, 2] == j)
            def _():
                pltpu.make_async_copy(
                    v_pieces[j].at[table[row, 3]], vf_ref.at[r], sems.at[1, r]
                ).start()

    q = q_ref[...]
    s = jnp.where(causal_mask(), dot(k_ref[...], q, 1, 1) * SCALING, -1e30)
    s_ref[0] = s
    peak = jnp.max(s, axis=0, keepdims=True)
    for r in range(LISTED):
        pltpu.make_async_copy(k_pieces[0].at[0], kf_ref.at[r], sems.at[0, r]).wait()
        bias = jnp.where(table[step * LISTED + r, 4] == 1, 0.0, -1e30).astype(F32)
        s = dot(kf_ref[r], q, 1, 1) * SCALING + bias
        s_ref[r + 1] = s
        peak = jnp.maximum(peak, jnp.max(s, axis=0, keepdims=True))
    total = jnp.zeros((1, BLOCK), F32)
    for r in range(LISTED + 1):
        e = jnp.exp(s_ref[r] - peak)
        s_ref[r] = e
        total = total + jnp.sum(e, axis=0, keepdims=True)
    inverse = 1.0 / total
    out = jnp.zeros((HD, BLOCK), F32)
    for r in range(LISTED + 1):
        p = (s_ref[r] * inverse).astype(BF)
        p_ref[0, r] = p
        if r == 0:
            value = v_ref[...]
        else:
            pltpu.make_async_copy(v_pieces[0].at[0], vf_ref.at[r - 1], sems.at[1, r - 1]).wait()
            value = vf_ref[r - 1]
        out = out + dot(value, p, 0, 0)
    out_ref[...] = out.T.astype(BF)


def sparse_forward(table, queries, keys, values, base, k_pieces, v_pieces):
    column = pl.BlockSpec(TILE, lambda i, t: (i, LIN))
    anywhere = pl.BlockSpec(memory_space=pl.ANY)
    return pl.pallas_call(
        sparse_forward_kernel,
        grid_spec=pltpu.PrefetchScalarGridSpec(
            num_scalar_prefetch=1,
            grid=(2,),
            in_specs=[column] * 3 + [anywhere] * 21,
            out_specs=[
                column,
                pl.BlockSpec((1, LISTED + 1, BLOCK, BLOCK), lambda i, t: (i, 0, 0, 0)),
                pl.BlockSpec((LISTED, BLOCK, HD), lambda i, t: (i, 0, 0)),
                pl.BlockSpec((LISTED, BLOCK, HD), lambda i, t: (i, 0, 0)),
            ],
            scratch_shapes=[
                pltpu.VMEM((LISTED + 1, BLOCK, BLOCK), F32),
                pltpu.SemaphoreType.DMA((2, LISTED)),
            ],
        ),
        out_shape=[
            jax.ShapeDtypeStruct(queries.shape, BF),
            jax.ShapeDtypeStruct((2, LISTED + 1, BLOCK, BLOCK), BF),
            jax.ShapeDtypeStruct((2 * LISTED, BLOCK, HD), BF),
            jax.ShapeDtypeStruct((2 * LISTED, BLOCK, HD), BF),
        ],
        input_output_aliases={4: 0},
        compiler_params=params(32),
        cost_estimate=cost(4e9, 12 * MIB),
        name="sparse_forward",
    )(table, queries, keys, values, base, *k_pieces, *v_pieces)


def sparse_backward_kernel(
    q_ref, k_ref, v_ref, g_ref, o_ref, p_ref, kf_ref, vf_ref, dq_ref, dk_ref, dv_ref, pk_ref, pv_ref
):
    q, g = q_ref[...], g_ref[...]
    row_dot = jnp.sum((g.astype(F32) * o_ref[...].astype(F32)).T, axis=0, keepdims=True)
    dq = jnp.zeros((HD, BLOCK), F32)
    for r in range(LISTED + 1):
        p = p_ref[0, r]
        key = k_ref[...] if r == 0 else kf_ref[r - 1]
        value = v_ref[...] if r == 0 else vf_ref[r - 1]
        dp = dot(value, g, 1, 1)
        ds = (p.astype(F32) * (dp - row_dot)).astype(BF)
        dq = dq + dot(key, ds, 0, 0)
        dk = dot(ds, q, 1, 0) * SCALING
        dv = dot(p, g, 1, 0)
        if r == 0:
            dk_ref[...] = dk
            dv_ref[...] = dv
        else:
            pk_ref[r - 1] = dk.astype(BF)
            pv_ref[r - 1] = dv.astype(BF)
    dq_ref[...] = (dq * SCALING).T.astype(BF)


def sparse_backward(queries, keys, values, grads, outs, probs, far_k, far_v):
    column = pl.BlockSpec(TILE, lambda i: (i, LIN))
    four = pl.BlockSpec((LISTED, BLOCK, HD), lambda i: (i, 0, 0))
    rows = pl.BlockSpec(TILE, lambda i: (i, 0))
    return pl.pallas_call(
        sparse_backward_kernel,
        grid=(2,),
        in_specs=[column] * 5
        + [pl.BlockSpec((1, LISTED + 1, BLOCK, BLOCK), lambda i: (i, 0, 0, 0)), four, four],
        out_specs=[column, rows, rows, four, four],
        out_shape=[
            jax.ShapeDtypeStruct(queries.shape, BF),
            jax.ShapeDtypeStruct((2 * BLOCK, HD), F32),
            jax.ShapeDtypeStruct((2 * BLOCK, HD), F32),
            jax.ShapeDtypeStruct((2 * LISTED, BLOCK, HD), BF),
            jax.ShapeDtypeStruct((2 * LISTED, BLOCK, HD), BF),
        ],
        compiler_params=params(32),
        cost_estimate=cost(8e9, 12 * MIB),
        name="sparse_backward",
    )(queries, keys, values, grads, outs, probs, far_k, far_v)


def placed(table, stream, j, own_ref, peer_ref):
    a, b = table[2 * stream, j], table[2 * stream + 1, j]
    first = own_ref[jnp.maximum(a, 0)].astype(F32) * jnp.where(a >= 0, 1.0, 0.0).astype(F32)
    second = peer_ref[jnp.maximum(b, 0)].astype(F32) * jnp.where(b >= 0, 1.0, 0.0).astype(F32)
    return first + second


def back_call(kernel, table, operands, shapes, name):
    vm = pl.BlockSpec(memory_space=pltpu.VMEM)
    nbytes = sum(math.prod(o.shape) * 2 for o in operands) + sum(math.prod(s) * 2 for s in shapes)
    return pl.pallas_call(
        kernel,
        in_specs=[pl.BlockSpec(memory_space=pltpu.SMEM)] + [vm] * len(operands),
        out_specs=[vm] * len(shapes),
        out_shape=[jax.ShapeDtypeStruct(s, BF) for s in shapes],
        compiler_params=params(32),
        cost_estimate=cost(1e7, nbytes),
        name=name,
    )(table, *operands)


def far_kernel(table, ok, pk, ov, pv, ka, kb, va, vb):
    for stream, own, peer, first, second in ((0, ok, pk, ka, kb), (1, ov, pv, va, vb)):

        @pl.loop(0, 4)
        def _(j):
            first[j] = placed(table, stream, 16 + j, own, peer).astype(BF)
            second[j] = placed(table, stream, 20 + j, own, peer).astype(BF)


def near_kernel(table, ok, pk, ov, pv, rka, rkb, rva, rvb, k1, k3, v1, v3):
    for stream, own, peer, ra, rb, right, left in (
        (0, ok, pk, rka, rkb, k1, k3),
        (1, ov, pv, rva, rvb, v1, v3),
    ):

        @pl.loop(0, 4)
        def _(j):
            right[j] = (placed(table, stream, 8 + j, own, peer) + ra[j].astype(F32)).astype(BF)
            right[j + 4] = placed(table, stream, 12 + j, own, peer).astype(BF)
            left[j] = placed(table, stream, 24 + j, own, peer).astype(BF)
            left[j + 4] = (placed(table, stream, 28 + j, own, peer) + rb[j].astype(F32)).astype(BF)


def turn_kernel(table, ok, pk, ov, pv, rka, rkb, rva, rvb, *outs):
    for stream, own, peer, ra, rb in ((0, ok, pk, rka, rkb), (1, ov, pv, rva, rvb)):
        home, right, far_a, far_b, left = outs[5 * stream : 5 * stream + 5]
        targets = [
            (home, 0), (home, 1), (right, 0), (right, 1), (far_a, 0), (far_b, 0), (left, 0), (left, 1)
        ]
        for j, (ref, w) in enumerate(targets):
            total = placed(table, stream, j, own, peer) + ra[j].astype(F32) + rb[j].astype(F32)
            ref[w] = total.astype(BF)


def last_kernel(kr, kl, vr, vl, rka, rkb, rva, rvb, okr, okl, ovr, ovl):
    for right, left, ra, rb, o_right, o_left in (
        (kr, kl, rka, rkb, okr, okl),
        (vr, vl, rva, rvb, ovr, ovl),
    ):
        o_right[0] = (right[0].astype(F32) + ra[0].astype(F32)).astype(BF)
        o_right[1] = right[1]
        o_left[0] = left[0]
        o_left[1] = (left[1].astype(F32) + rb[0].astype(F32)).astype(BF)


def last_sums(operands):
    vm = pl.BlockSpec(memory_space=pltpu.VMEM)
    return pl.pallas_call(
        last_kernel,
        in_specs=[vm] * 8,
        out_specs=[vm] * 4,
        out_shape=[jax.ShapeDtypeStruct((2, BLOCK, HD), BF)] * 4,
        compiler_params=params(16),
        cost_estimate=cost(1e6, 2 * MIB),
        name="last_sums",
    )(*operands)


def finish_kernel(dk, dv, k0, ka, kb, v0, va, vb, kg_in, vg_in, kg, vg):
    kg[...] = (dk[...] + k0[0].astype(F32) + ka[0].astype(F32) + kb[0].astype(F32)).astype(BF)
    vg[...] = (dv[...] + v0[0].astype(F32) + va[0].astype(F32) + vb[0].astype(F32)).astype(BF)


def finish(dk, dv, pieces, key_grad, value_grad):
    rows = pl.BlockSpec(TILE, lambda i: (i, 0))
    piece = pl.BlockSpec((1, BLOCK, HD), lambda i: (i, 0, 0))
    column = pl.BlockSpec(TILE, lambda i: (i, LIN))
    anywhere = pl.BlockSpec(memory_space=pl.ANY)
    shape = jax.ShapeDtypeStruct(key_grad.shape, BF)
    return pl.pallas_call(
        finish_kernel,
        grid=(2,),
        in_specs=[rows, rows] + [piece] * 6 + [anywhere] * 2,
        out_specs=[column, column],
        out_shape=[shape, shape],
        input_output_aliases={8: 0, 9: 1},
        compiler_params=params(16),
        cost_estimate=cost(1e6, 3 * MIB),
        name="finish",
    )(dk, dv, *pieces, key_grad, value_grad)


def return_sums(pair_k, pair_v, table):
    peer_k, peer_v = swap(pair_k), swap(pair_v)
    base = [pair_k, peer_k, pair_v, peer_v]
    zmove, xmove = along("z"), along("x")
    four, eight = (4, BLOCK, HD), (8, BLOCK, HD)
    ka, kb, va, vb = back_call(far_kernel, table, base, [four] * 4, "back_far")
    got = [zmove(ka, 1), zmove(kb, -1), xmove(va, 1), xmove(vb, -1)]
    k1, k3, v1, v3 = back_call(near_kernel, table, base + got, [eight] * 4, "back_near")
    got = [zmove(k1, 1), zmove(k3, -1), xmove(v1, 1), xmove(v3, -1)]
    two, one = (2, BLOCK, HD), (1, BLOCK, HD)
    outs = back_call(turn_kernel, table, base + got, [two, two, one, one, two] * 2, "back_turn")
    k0, k1, ka, kb, k3, v0, v1, va, vb, v3 = outs
    got = [xmove(ka, 1), xmove(kb, -1), zmove(va, 1), zmove(vb, -1)]
    k1, k3, v1, v3 = last_sums([k1, k3, v1, v3] + got)
    return [k0, xmove(k1, 1), xmove(k3, -1), v0, zmove(v1, 1), zmove(v3, -1)]


def where_is(blocks, place):
    owner, within = blocks // 2, blocks % 2
    pz = (place // (SIDE * CORES) - owner // (SIDE * CORES)) % SIDE
    px = (place // CORES % SIDE - owner // CORES % SIDE) % SIDE
    return pz, px, owner % CORES, within


def piece_of(outer, inner, within, peer):
    second = (outer == 2) & (inner >= 2)
    piece = jnp.where(outer < 2, outer, jnp.where(outer == 3, 4, jnp.where(second, 3, 2)))
    index = inner * 2 + within - jnp.where(second, 4, 0)
    return piece + 5 * peer, index


def fetch_table(lists, place):
    flat = lists.reshape(-1)
    pz, px, core, within = where_is(flat, place)
    peer = (core != place % CORES).astype(jnp.int32)
    k_piece, k_index = piece_of(pz, px, within, peer)
    v_piece, v_index = piece_of(px, pz, within, peer)
    mine = place * 2 + jnp.arange(2 * LISTED, dtype=jnp.int32) // LISTED
    usable = (flat != mine).astype(jnp.int32)
    return jnp.stack([k_piece, k_index, v_piece, v_index, usable], axis=1).astype(jnp.int32)


def back_table(lists, peer_lists, place):
    slots = jnp.arange(2 * LISTED, dtype=jnp.int32)[:, None]
    spots = jnp.arange(32, dtype=jnp.int32)[None, :]
    rows = []
    for outer_z in (True, False):
        for some in (lists, peer_lists):
            pz, px, core, within = where_is(some.reshape(-1), place)
            pz, px = (-pz) % SIDE, (-px) % SIDE
            outer, inner = (pz, px) if outer_z else (px, pz)
            target = jnp.where(core == place % CORES, (outer * SIDE + inner) * 2 + within, -1)
            rows.append(jnp.max(jnp.where(target[:, None] == spots, slots, -1), axis=0))
    return jnp.stack(rows).astype(jnp.int32)


def split(value):
    high = value.astype(BF)
    return high, (value - high.astype(F32)).astype(BF)


def local(queries, keys, values, out_weight, out_grad, long_blocks):
    place = lax.axis_index("ctx")
    row_count = queries.shape[0]
    positions = place * row_count + jnp.arange(row_count, dtype=jnp.int32)
    scale = 1.0 / (math.sqrt(HD) * jnp.sqrt((positions + 1).astype(F32)))
    scale = jnp.broadcast_to(scale[None, :], (8, row_count))
    lists = lax.dynamic_slice_in_dim(long_blocks, place * 2, 2, 0)
    peer_lists = lax.dynamic_slice_in_dim(long_blocks, (place ^ 1) * 2, 2, 0)
    fetch = fetch_table(lists, place)
    back = back_table(lists, peer_lists, place)

    grad_all = lax.all_gather(out_grad, "head", axis=1, tiled=True)

    own_k = keys[:, LIN * HD :].reshape(2, BLOCK, HD)
    own_v = values[:, LIN * HD :].reshape(2, BLOCK, HD)
    line_k = ring_gather(own_k, "x")
    line_v = ring_gather(own_v, "z")
    k_pieces = ring_gather(jnp.concatenate(line_k, axis=0), "z")
    v_pieces = ring_gather(jnp.concatenate(line_v, axis=0), "x")
    k_pieces = k_pieces + [swap(p) for p in k_pieces]
    v_pieces = v_pieces + [swap(p) for p in v_pieces]

    states = block_states(keys, values)
    before = scan_states(states[0] + states[1], False)
    before = jnp.stack([before, before + states[0]])
    flip_hi, flip_lo = split(jnp.swapaxes(before, 2, 3))
    attention = linear_forward(queries, keys, values, scale, flip_hi, flip_lo)
    attention, probs, far_k, far_v = sparse_forward(
        fetch, queries, keys, values, attention, k_pieces, v_pieces
    )
    partial_out = dot(attention, out_weight, 1, 1).astype(BF)
    layer_out = lax.psum_scatter(partial_out, "head", scatter_dimension=1, tiled=True)

    attn_grad = dot(grad_all, out_weight, 1, 0).astype(BF)
    query_grad, own_dk, own_dv, pair_k, pair_v = sparse_backward(
        queries, keys, values, attn_grad, attention, probs, far_k, far_v
    )
    pieces = return_sums(pair_k, pair_v, back)

    adjoints = block_adjoints(queries, attn_grad, scale)
    after = scan_states(adjoints[0] + adjoints[1], True)
    after = jnp.stack([after + adjoints[1], after])
    query_grad, key_grad, value_grad = linear_backward(
        queries, keys, values, attn_grad, scale, *split(before), *split(after), query_grad
    )
    key_grad, value_grad = finish(own_dk, own_dv, pieces, key_grad, value_grad)
    return layer_out, query_grad, key_grad, value_grad


def solution(mesh):
    return jax.shard_map(
        local,
        mesh=mesh,
        in_specs=(
            P("ctx", "head"),
            P("ctx", "head"),
            P("ctx", "head"),
            P(None, "head"),
            P("ctx", "head"),
            P(),
        ),
        out_specs=(P("ctx", "head"), P("ctx", "head"), P("ctx", "head"), P("ctx", "head")),
        check_vma=False,
    )
```

```python
import functools
import math

import jax
import jax.numpy as jnp
from jax import lax
from jax.experimental import pallas as pl
from jax.experimental.pallas import tpu as pltpu
from jax.sharding import PartitionSpec as P

HD = 128
LIN = 3
LISTED = 4
BLOCK = 512
SIDE = 4
CORES = 2
CTX = SIDE * SIDE * CORES
SCALING = 1.0 / math.sqrt(HD)
BF = jnp.bfloat16
F32 = jnp.float32
MIB = 1 << 20
TILE = (BLOCK, HD)


def dot(a, b, ca, cb):
    return lax.dot_general(a, b, (((ca,), (cb,)), ((), ())), preferred_element_type=F32)


def params(mib):
    return pltpu.CompilerParams(vmem_limit_bytes=mib * MIB)


def cost(flops, nbytes):
    return pl.CostEstimate(flops=int(flops), bytes_accessed=int(nbytes), transcendentals=0)


def ring_move(value, axis, step):
    pairs = []
    for z in range(SIDE):
        for x in range(SIDE):
            for c in range(CORES):
                dx, dz = (step, 0) if axis == c else (0, step)
                to = (((z + dz) % SIDE) * SIDE + (x + dx) % SIDE) * CORES + c
                pairs.append(((z * SIDE + x) * CORES + c, to))
    return lax.ppermute(value, "ctx", pairs)


def swap(value):
    return lax.ppermute(value, "ctx", [(i, i ^ 1) for i in range(CTX)])


def head_move(value, step):
    return lax.ppermute(value, "head", [(i, (i + step) % SIDE) for i in range(SIDE)])


def after(value, *others):
    return lax.optimization_barrier((value, *others))[0]


def scan_step(own, total, step, backward):
    if backward:
        pairs = [(i + step, i) for i in range(CTX - step)]
    else:
        pairs = [(i, i + step) for i in range(CTX - step)]
    return lax.ppermute((own + total).astype(BF), "ctx", pairs)


def copies_kernel(moves, n_in, *refs):
    ins, outs, sems = refs[:n_in], refs[n_in:-1], refs[-1]
    copies = [
        pltpu.make_async_copy(
            ins[i].at[pl.ds(i0, n)], outs[o].at[pl.ds(o0, n)], sems.at[m]
        )
        for m, (i, i0, o, o0, n) in enumerate(moves)
    ]
    for copy in copies:
        copy.start()
    for copy in copies:
        copy.wait()


def copies(inputs, sizes, moves):
    anywhere = pl.BlockSpec(memory_space=pl.ANY)
    return pl.pallas_call(
        functools.partial(copies_kernel, moves, len(inputs)),
        in_specs=[anywhere] * len(inputs),
        out_specs=[anywhere] * len(sizes),
        out_shape=[jax.ShapeDtypeStruct((n,) + inputs[0].shape[1:], BF) for n in sizes],
        scratch_shapes=[pltpu.SemaphoreType.DMA((len(moves),))],
        compiler_params=params(4),
        cost_estimate=cost(0, sum(m[4] for m in moves) * math.prod(inputs[0].shape[1:]) * 4),
        name="copies",
    )(*inputs)


def joined(pieces):
    moves, spot = [], 0
    for i, piece in enumerate(pieces):
        moves.append((i, 0, 0, spot, piece.shape[0]))
        spot += piece.shape[0]
    return copies(pieces, [spot], moves)[0]


def halves(right, left):
    n = right.shape[0] // 2
    return copies([right, left], [n, n], [(0, 0, 0, 0, n), (1, n, 1, 0, n)])


def causal_mask():
    s = lax.broadcasted_iota(jnp.int32, (BLOCK, BLOCK), 0)
    u = lax.broadcasted_iota(jnp.int32, (BLOCK, BLOCK), 1)
    return s <= u


def states_kernel(k_ref, v_ref, out_ref):
    out_ref[0, 0] = dot(k_ref[...], v_ref[...], 0, 0)


def adjoint_kernel(q_ref, g_ref, c_ref, out_ref):
    qt = (q_ref[...].astype(F32).T * c_ref[0:1, :]).astype(BF)
    out_ref[0, 0] = dot(qt, g_ref[...], 1, 0)


def tile_spec():
    return pl.BlockSpec(TILE, lambda i, h: (i, h))


def scale_spec():
    return pl.BlockSpec((8, BLOCK), lambda i, h: (0, i))


def state_spec():
    return pl.BlockSpec((1, 1, HD, HD), lambda i, h: (i, h, 0, 0))


def block_states(keys, values):
    return pl.pallas_call(
        states_kernel,
        grid=(2, LIN),
        in_specs=[tile_spec(), tile_spec()],
        out_specs=state_spec(),
        out_shape=jax.ShapeDtypeStruct((2, LIN, HD, HD), F32),
        compiler_params=params(16),
        cost_estimate=cost(1e8, 2 * MIB),
        name="block_states",
    )(keys, values)


def block_adjoints(queries, grads, scale):
    return pl.pallas_call(
        adjoint_kernel,
        grid=(2, LIN),
        in_specs=[tile_spec(), tile_spec(), scale_spec()],
        out_specs=state_spec(),
        out_shape=jax.ShapeDtypeStruct((2, LIN, HD, HD), F32),
        compiler_params=params(16),
        cost_estimate=cost(1e8, 2 * MIB),
        name="block_adjoints",
    )(queries, grads, scale)


def linear_forward_kernel(q_ref, k_ref, v_ref, c_ref, hi_ref, lo_ref, out_ref):
    q, k, v, c = q_ref[...], k_ref[...], v_ref[...], c_ref[0:1, :]
    weights = jnp.where(causal_mask(), dot(k, q, 1, 1) * c, 0.0).astype(BF)
    out = dot(v, weights, 0, 0)
    out = out + c * (dot(hi_ref[0, 0], q, 1, 1) + dot(lo_ref[0, 0], q, 1, 1))
    out_ref[...] = out.T.astype(BF)


def linear_forward(queries, keys, values, scale, hi, lo):
    return pl.pallas_call(
        linear_forward_kernel,
        grid=(2, LIN),
        in_specs=[tile_spec()] * 3 + [scale_spec(), state_spec(), state_spec()],
        out_specs=tile_spec(),
        out_shape=jax.ShapeDtypeStruct(queries.shape, BF),
        compiler_params=params(24),
        cost_estimate=cost(2.4e9, 4 * MIB),
        name="linear_forward",
    )(queries, keys, values, scale, hi, lo)


def linear_backward_kernel(
    q_ref, k_ref, v_ref, g_ref, c_ref, sh_ref, sl_ref, ah_ref, al_ref, base_ref, dq_ref, dk_ref, dv_ref
):
    q, k, v, g, c = q_ref[...], k_ref[...], v_ref[...], g_ref[...], c_ref[0:1, :]
    mask = causal_mask()
    grad_weights = jnp.where(mask, dot(v, g, 1, 1) * c, 0.0).astype(BF)
    dq = dot(k, grad_weights, 0, 0)
    dq = dq + c * (dot(sh_ref[0, 0], g, 1, 1) + dot(sl_ref[0, 0], g, 1, 1))
    dq_ref[...] = dq.T.astype(BF)
    dk = dot(grad_weights, q, 1, 0) + dot(v, ah_ref[0, 0], 1, 1) + dot(v, al_ref[0, 0], 1, 1)
    dk_ref[...] = dk.astype(BF)
    weights = jnp.where(mask, dot(k, q, 1, 1) * c, 0.0).astype(BF)
    dv = dot(weights, g, 1, 0) + dot(k, ah_ref[0, 0], 1, 0) + dot(k, al_ref[0, 0], 1, 0)
    dv_ref[...] = dv.astype(BF)


def linear_backward(queries, keys, values, grads, scale, sh, sl, ah, al, base):
    shape = jax.ShapeDtypeStruct(queries.shape, BF)
    return pl.pallas_call(
        linear_backward_kernel,
        grid=(2, LIN),
        in_specs=[tile_spec()] * 4
        + [scale_spec()]
        + [state_spec()] * 4
        + [pl.BlockSpec(memory_space=pl.ANY)],
        out_specs=[tile_spec()] * 3,
        out_shape=[shape] * 3,
        input_output_aliases={9: 0},
        compiler_params=params(24),
        cost_estimate=cost(5e9, 8 * MIB),
        name="linear_backward",
    )(queries, keys, values, grads, scale, sh, sl, ah, al, base)


def sparse_forward_kernel(table, q_ref, k_ref, v_ref, base_ref, *rest):
    pieces = rest[:10]
    out_ref, p_ref, kf_ref, vf_ref, s_ref, sems = rest[10:]
    step = pl.program_id(0)
    for r in range(LISTED):
        row = step * LISTED + r
        for j in range(10):

            @pl.when(table[row, 0] == j)
            def _():
                pltpu.make_async_copy(pieces[j].at[table[row, 1]], kf_ref.at[r], sems.at[0, r]).start()

            @pl.when(table[row, 2] == j)
            def _():
                pltpu.make_async_copy(pieces[j].at[table[row, 3]], vf_ref.at[r], sems.at[1, r]).start()

    q = q_ref[...]
    s = jnp.where(causal_mask(), dot(k_ref[...], q, 1, 1) * SCALING, -1e30)
    s_ref[0] = s
    peak = jnp.max(s, axis=0, keepdims=True)
    for r in range(LISTED):
        pltpu.make_async_copy(pieces[0].at[0], kf_ref.at[r], sems.at[0, r]).wait()
        bias = jnp.where(table[step * LISTED + r, 4] == 1, 0.0, -1e30).astype(F32)
        s = dot(kf_ref[r], q, 1, 1) * SCALING + bias
        s_ref[r + 1] = s
        peak = jnp.maximum(peak, jnp.max(s, axis=0, keepdims=True))
    total = jnp.zeros((1, BLOCK), F32)
    for r in range(LISTED + 1):
        e = jnp.exp(s_ref[r] - peak)
        s_ref[r] = e
        total = total + jnp.sum(e, axis=0, keepdims=True)
    inverse = 1.0 / total
    out = jnp.zeros((HD, BLOCK), F32)
    for r in range(LISTED + 1):
        p = (s_ref[r] * inverse).astype(BF)
        p_ref[0, r] = p
        if r == 0:
            value = v_ref[...]
        else:
            pltpu.make_async_copy(pieces[0].at[0], vf_ref.at[r - 1], sems.at[1, r - 1]).wait()
            value = vf_ref[r - 1]
        out = out + dot(value, p, 0, 0)
    out_ref[...] = out.T.astype(BF)


def sparse_forward(table, queries, keys, values, base, pieces):
    column = pl.BlockSpec(TILE, lambda i, t: (i, LIN))
    anywhere = pl.BlockSpec(memory_space=pl.ANY)
    return pl.pallas_call(
        sparse_forward_kernel,
        grid_spec=pltpu.PrefetchScalarGridSpec(
            num_scalar_prefetch=1,
            grid=(2,),
            in_specs=[column] * 3 + [anywhere] * 11,
            out_specs=[
                column,
                pl.BlockSpec((1, LISTED + 1, BLOCK, BLOCK), lambda i, t: (i, 0, 0, 0)),
                pl.BlockSpec((LISTED, BLOCK, HD), lambda i, t: (i, 0, 0)),
                pl.BlockSpec((LISTED, BLOCK, HD), lambda i, t: (i, 0, 0)),
            ],
            scratch_shapes=[
                pltpu.VMEM((LISTED + 1, BLOCK, BLOCK), F32),
                pltpu.SemaphoreType.DMA((2, LISTED)),
            ],
        ),
        out_shape=[
            jax.ShapeDtypeStruct(queries.shape, BF),
            jax.ShapeDtypeStruct((2, LISTED + 1, BLOCK, BLOCK), BF),
            jax.ShapeDtypeStruct((2 * LISTED, BLOCK, HD), BF),
            jax.ShapeDtypeStruct((2 * LISTED, BLOCK, HD), BF),
        ],
        input_output_aliases={4: 0},
        compiler_params=params(32),
        cost_estimate=cost(4e9, 12 * MIB),
        name="sparse_forward",
    )(table, queries, keys, values, base, *pieces)


def sparse_backward_kernel(
    core, q_ref, k_ref, v_ref, g_ref, o_ref, p_ref, kf_ref, vf_ref, dq_ref, dk_ref, dv_ref, mine_ref, sent_ref
):
    first = core[0] == 0
    q, g = q_ref[...], g_ref[...]
    row_dot = jnp.sum((g.astype(F32) * o_ref[...].astype(F32)).T, axis=0, keepdims=True)
    dq = jnp.zeros((HD, BLOCK), F32)
    for r in range(LISTED + 1):
        p = p_ref[0, r]
        key = k_ref[...] if r == 0 else kf_ref[r - 1]
        value = v_ref[...] if r == 0 else vf_ref[r - 1]
        dp = dot(value, g, 1, 1)
        ds = (p.astype(F32) * (dp - row_dot)).astype(BF)
        dq = dq + dot(key, ds, 0, 0)
        dk = dot(ds, q, 1, 0) * SCALING
        dv = dot(p, g, 1, 0)
        if r == 0:
            dk_ref[...] = dk
            dv_ref[...] = dv
        else:
            mine_ref[r - 1] = jnp.where(first, dk, dv).astype(BF)
            sent_ref[r - 1] = jnp.where(first, dv, dk).astype(BF)
    dq_ref[...] = (dq * SCALING).T.astype(BF)


def sparse_backward(core, queries, keys, values, grads, outs, probs, far_k, far_v):
    column = pl.BlockSpec(TILE, lambda i, c: (i, LIN))
    four = pl.BlockSpec((LISTED, BLOCK, HD), lambda i, c: (i, 0, 0))
    rows = pl.BlockSpec(TILE, lambda i, c: (i, 0))
    five = pl.BlockSpec((1, LISTED + 1, BLOCK, BLOCK), lambda i, c: (i, 0, 0, 0))
    return pl.pallas_call(
        sparse_backward_kernel,
        grid_spec=pltpu.PrefetchScalarGridSpec(
            num_scalar_prefetch=1,
            grid=(2,),
            in_specs=[column] * 5 + [five, four, four],
            out_specs=[column, rows, rows, four, four],
        ),
        out_shape=[
            jax.ShapeDtypeStruct(queries.shape, BF),
            jax.ShapeDtypeStruct((2 * BLOCK, HD), F32),
            jax.ShapeDtypeStruct((2 * BLOCK, HD), F32),
            jax.ShapeDtypeStruct((2 * LISTED, BLOCK, HD), BF),
            jax.ShapeDtypeStruct((2 * LISTED, BLOCK, HD), BF),
        ],
        compiler_params=params(32),
        cost_estimate=cost(8e9, 12 * MIB),
        name="sparse_backward",
    )(core, queries, keys, values, grads, outs, probs, far_k, far_v)


def choose_kernel(core, k_ref, v_ref, mine_ref, sent_ref):
    first = core[0] == 0
    k, v = k_ref[...], v_ref[...]
    mine_ref[0] = jnp.where(first, k, v)
    sent_ref[0] = jnp.where(first, v, k)


def choose(core, keys, values):
    column = pl.BlockSpec(TILE, lambda i, c: (i, LIN))
    block = pl.BlockSpec((1, BLOCK, HD), lambda i, c: (i, 0, 0))
    return pl.pallas_call(
        choose_kernel,
        grid_spec=pltpu.PrefetchScalarGridSpec(
            num_scalar_prefetch=1, grid=(2,), in_specs=[column] * 2, out_specs=[block] * 2
        ),
        out_shape=[jax.ShapeDtypeStruct((2, BLOCK, HD), BF)] * 2,
        compiler_params=params(4),
        cost_estimate=cost(1e6, MIB),
        name="choose",
    )(core, keys, values)


ROWS = 256


def grad_near_kernel(order, own, right, left, w0, w3, w1, out):
    out[...] = (
        dot(own[...], w0[...], 1, 0) + dot(right[...], w3[...], 1, 0) + dot(left[...], w1[...], 1, 0)
    )


def weight_spec(shape, nth):
    return pl.BlockSpec(shape, lambda i, o: (o[nth], 0))


def grad_near(order, own, right, left, weight):
    rows, width = own.shape
    cols = weight.shape[1]
    part = pl.BlockSpec((ROWS, width), lambda i, o: (i, 0))
    return pl.pallas_call(
        grad_near_kernel,
        grid_spec=pltpu.PrefetchScalarGridSpec(
            num_scalar_prefetch=1,
            grid=(rows // ROWS,),
            in_specs=[part] * 3 + [weight_spec((width, cols), n) for n in (0, 3, 1)],
            out_specs=pl.BlockSpec((ROWS, cols), lambda i, o: (i, 0)),
        ),
        out_shape=jax.ShapeDtypeStruct((rows, cols), F32),
        compiler_params=params(32),
        cost_estimate=cost(6 * rows * width * cols, 11 * MIB),
        name="grad_near",
    )(order, own, right, left, weight, weight, weight)


def low(i):
    return jnp.minimum(i, 1)


def high(i):
    return jnp.maximum(i - 2, 0)


def grad_far_kernel(order, part, far_a, far_b, w2, out):
    far = jnp.where(pl.program_id(0) < 2, far_a[...], far_b[...])
    out[...] = (part[...] + dot(far, w2[...], 1, 0)).astype(BF)


def grad_far(order, part, far_a, far_b, weight):
    rows, cols = part.shape
    width = far_a.shape[1]
    tile = pl.BlockSpec((ROWS, cols), lambda i, o: (i, 0))
    return pl.pallas_call(
        grad_far_kernel,
        grid_spec=pltpu.PrefetchScalarGridSpec(
            num_scalar_prefetch=1,
            grid=(rows // ROWS,),
            in_specs=[
                tile,
                pl.BlockSpec((ROWS, width), lambda i, o: (low(i), 0)),
                pl.BlockSpec((ROWS, width), lambda i, o: (high(i), 0)),
                weight_spec((width, cols), 2),
            ],
            out_specs=tile,
        ),
        out_shape=jax.ShapeDtypeStruct((rows, cols), BF),
        compiler_params=params(32),
        cost_estimate=cost(2 * rows * width * cols, 6 * MIB),
        name="grad_far",
    )(order, part, far_a, far_b, weight)


def out_far_kernel(order, a, w, far_a, far_b):
    value = dot(a[...], w[...], 1, 1).astype(BF)

    @pl.when(pl.program_id(0) < 2)
    def _():
        far_a[...] = value

    @pl.when(pl.program_id(0) >= 2)
    def _():
        far_b[...] = value


def out_near_kernel(order, a, w1, w3, ra, rb, n1, n3):
    first = pl.program_id(0) < 2
    more = jnp.where(first, ra[...], 0).astype(F32)
    n1[...] = (dot(a[...], w1[...], 1, 1) + more).astype(BF)
    more = jnp.where(first, 0, rb[...]).astype(F32)
    n3[...] = (dot(a[...], w3[...], 1, 1) + more).astype(BF)


def out_home_kernel(order, a, w0, r1, r3, out):
    out[...] = (dot(a[...], w0[...], 1, 1) + r1[...].astype(F32) + r3[...].astype(F32)).astype(BF)


def out_call(kernel, order, attention, weight, nths, others, other_maps, out_rows, out_maps, name):
    rows, cols = attention.shape
    width = weight.shape[0] // SIDE

    def spec(index):
        return pl.BlockSpec((ROWS, width), lambda i, o: (index(i), 0))

    return pl.pallas_call(
        kernel,
        grid_spec=pltpu.PrefetchScalarGridSpec(
            num_scalar_prefetch=1,
            grid=(rows // ROWS,),
            in_specs=[pl.BlockSpec((ROWS, cols), lambda i, o: (i, 0))]
            + [weight_spec((width, cols), n) for n in nths]
            + [spec(m) for m in other_maps],
            out_specs=[spec(m) for m in out_maps],
        ),
        out_shape=[jax.ShapeDtypeStruct((r, width), BF) for r in out_rows],
        compiler_params=params(32),
        cost_estimate=cost(2 * len(nths) * rows * width * cols, (3 + 2 * len(out_rows)) * MIB),
        name=name,
    )(order, attention, *([weight] * len(nths)), *others)


def same(i):
    return i


def placed(table, j, own_ref, peer_ref):
    a, b = table[0, j], table[1, j]
    first = own_ref[jnp.maximum(a, 0)].astype(F32) * jnp.where(a >= 0, 1.0, 0.0).astype(F32)
    second = peer_ref[jnp.maximum(b, 0)].astype(F32) * jnp.where(b >= 0, 1.0, 0.0).astype(F32)
    return first + second


def back_call(kernel, table, operands, sizes, name):
    vm = pl.BlockSpec(memory_space=pltpu.VMEM)
    shapes = [(n, BLOCK, HD) for n in sizes]
    nbytes = sum(math.prod(o.shape) * 2 for o in operands) + sum(math.prod(s) * 2 for s in shapes)
    return pl.pallas_call(
        kernel,
        in_specs=[pl.BlockSpec(memory_space=pltpu.SMEM)] + [vm] * len(operands),
        out_specs=[vm] * len(shapes),
        out_shape=[jax.ShapeDtypeStruct(s, BF) for s in shapes],
        compiler_params=params(32),
        cost_estimate=cost(1e7, nbytes),
        name=name,
    )(table, *operands)


def far_kernel(table, own, peer, far_a, far_b):
    @pl.loop(0, 8)
    def _(j):
        far_a[j] = placed(table, 32 + j, own, peer).astype(BF)
        far_b[j] = placed(table, 40 + j, own, peer).astype(BF)


def near_kernel(table, own, peer, ra, rb, right, left):
    @pl.loop(0, 8)
    def _(j):
        right[j] = (placed(table, 16 + j, own, peer) + ra[j].astype(F32)).astype(BF)
        right[j + 8] = placed(table, 24 + j, own, peer).astype(BF)
        left[j] = placed(table, 48 + j, own, peer).astype(BF)
        left[j + 8] = (placed(table, 56 + j, own, peer) + rb[j].astype(F32)).astype(BF)


def turn_kernel(table, own, peer, r1, r3, home, right, far_a, far_b, left):
    def total(j):
        return (placed(table, j, own, peer) + r1[j].astype(F32) + r3[j].astype(F32)).astype(BF)

    @pl.loop(0, 4)
    def _(j):
        home[j] = total(j)
        right[j] = total(4 + j)
        left[j] = total(12 + j)

    @pl.loop(0, 2)
    def _(j):
        far_a[j] = total(8 + j)
        far_b[j] = total(10 + j)


def last_kernel(table, right, left, ra, rb, o_right, o_left):
    for j in range(2):
        o_right[j] = (right[j].astype(F32) + ra[j].astype(F32)).astype(BF)
        o_right[j + 2] = right[j + 2]
        o_left[j] = left[j]
        o_left[j + 2] = (left[j + 2].astype(F32) + rb[j].astype(F32)).astype(BF)


def tail_kernel(table, home, r1, r3, mine, sent):
    for j in range(2):
        mine[j] = (home[j].astype(F32) + r1[j].astype(F32) + r3[j].astype(F32)).astype(BF)
        sent[j] = (home[j + 2].astype(F32) + r1[j + 2].astype(F32) + r3[j + 2].astype(F32)).astype(BF)


def finish_kernel(core, dk, dv, mine_ref, got_ref, kg_in, vg_in, kg, vg):
    first = core[0] == 0
    mine, got = mine_ref[0].astype(F32), got_ref[0].astype(F32)
    kg[...] = (dk[...] + jnp.where(first, mine, got)).astype(BF)
    vg[...] = (dv[...] + jnp.where(first, got, mine)).astype(BF)


def finish(core, dk, dv, mine, got, key_grad, value_grad):
    rows = pl.BlockSpec(TILE, lambda i, c: (i, 0))
    piece = pl.BlockSpec((1, BLOCK, HD), lambda i, c: (i, 0, 0))
    column = pl.BlockSpec(TILE, lambda i, c: (i, LIN))
    anywhere = pl.BlockSpec(memory_space=pl.ANY)
    shape = jax.ShapeDtypeStruct(key_grad.shape, BF)
    return pl.pallas_call(
        finish_kernel,
        grid_spec=pltpu.PrefetchScalarGridSpec(
            num_scalar_prefetch=1,
            grid=(2,),
            in_specs=[rows, rows, piece, piece, anywhere, anywhere],
            out_specs=[column, column],
        ),
        out_shape=[shape, shape],
        input_output_aliases={5: 0, 6: 1},
        compiler_params=params(16),
        cost_estimate=cost(1e6, 3 * MIB),
        name="finish",
    )(core, dk, dv, mine, got, key_grad, value_grad)


def where_is(blocks, place):
    owner, within = blocks // 2, blocks % 2
    pz = (place // (SIDE * CORES) - owner // (SIDE * CORES)) % SIDE
    px = (place // CORES % SIDE - owner // CORES % SIDE) % SIDE
    return pz, px, owner % CORES, within


def spot_of(blocks, place, stream):
    pz, px, core, within = where_is(blocks, place)
    rel = (core != stream).astype(jnp.int32)
    outer = jnp.where(stream == 0, pz, px)
    first = jnp.where(stream == 0, px, pz)
    return outer, first, rel * 2 + within


def piece_of(blocks, place, stream):
    outer, first, rest = spot_of(blocks, place, stream)
    second = (outer == 2) & (first >= 2)
    piece = jnp.where(outer < 2, outer, jnp.where(outer == 3, 4, jnp.where(second, 3, 2)))
    index = first * 4 + rest - jnp.where(second, 8, 0)
    return piece + 5 * (place % CORES != stream).astype(jnp.int32), index


def fetch_table(lists, place):
    flat = lists.reshape(-1)
    mine = place * 2 + jnp.arange(2 * LISTED, dtype=jnp.int32) // LISTED
    usable = (flat != mine).astype(jnp.int32)
    columns = [*piece_of(flat, place, 0), *piece_of(flat, place, 1), usable]
    return jnp.stack(columns, axis=1).astype(jnp.int32)


def back_table(lists, peer_lists, place):
    slots = jnp.arange(2 * LISTED, dtype=jnp.int32)[:, None]
    spots = jnp.arange(64, dtype=jnp.int32)[None, :]
    rows = []
    for some in (lists, peer_lists):
        outer, first, rest = spot_of(some.reshape(-1), place, place % CORES)
        target = (-outer) % SIDE * 16 + (-first) % SIDE * 4 + rest
        rows.append(jnp.max(jnp.where(target[:, None] == spots, slots, -1), axis=0))
    return jnp.stack(rows).astype(jnp.int32)


def split(value):
    high = value.astype(BF)
    return high, (value - high.astype(F32)).astype(BF)


def local(queries, keys, values, out_weight, out_grad, long_blocks):
    place = lax.axis_index("ctx")
    core = (place % CORES).astype(jnp.int32).reshape(1)
    order = (lax.axis_index("head") + jnp.arange(SIDE, dtype=jnp.int32)) % SIDE
    row_count = queries.shape[0]
    positions = place * row_count + jnp.arange(row_count, dtype=jnp.int32)
    scale = 1.0 / (math.sqrt(HD) * jnp.sqrt((positions + 1).astype(F32)))
    scale = jnp.broadcast_to(scale[None, :], (8, row_count))
    lists = lax.dynamic_slice_in_dim(long_blocks, place * 2, 2, 0)
    peer_lists = lax.dynamic_slice_in_dim(long_blocks, (place ^ 1) * 2, 2, 0)
    fetch = fetch_table(lists, place)
    back = back_table(lists, peer_lists, place)

    og_right, og_left = head_move(out_grad, 1), head_move(out_grad, -1)
    mine, sent = choose(core, keys, values)
    start = joined([mine, swap(sent)])
    a_right, a_left = ring_move(start, 0, 1), ring_move(start, 0, -1)
    cut = halves(a_right, a_left)
    a_far = ring_move(cut[0], 0, 1), ring_move(cut[1], 0, -1)
    line = joined([start, a_right, a_far[0], a_far[1], a_left])
    b_right, b_left = ring_move(line, 1, 1), ring_move(line, 1, -1)
    line_swapped = swap(line)
    cut = halves(b_right, b_left)
    b_far = ring_move(cut[0], 1, 1), ring_move(cut[1], 1, -1)
    pieces = [line, b_right, b_far[0], b_far[1], b_left]
    pieces = pieces + [line_swapped] + [swap(p) for p in pieces[1:]]

    grad_part = grad_near(order, out_grad, og_right, og_left, out_weight)
    rows = row_count // 2
    og_far = head_move(og_right[:rows], 1), head_move(og_left[rows:], -1)

    states = block_states(keys, values)
    own = states[0] + states[1]
    total = jnp.zeros_like(own)
    total = total + scan_step(own, total, 1, False).astype(F32)
    total = total + scan_step(own, total, 2, False).astype(F32)
    total = after(total, a_right, a_left)
    total = total + after(scan_step(own, total, 4, False), line).astype(F32)
    total = after(total, line_swapped)
    total = total + after(scan_step(own, total, 8, False), b_right, b_left).astype(F32)
    total = total + after(scan_step(own, total, 16, False), *b_far).astype(F32)
    before = jnp.stack([total, total + states[0]])
    flip_hi, flip_lo = split(jnp.swapaxes(before, 2, 3))

    attention = linear_forward(queries, keys, values, scale, flip_hi, flip_lo)
    attention, probs, far_k, far_v = sparse_forward(
        fetch, queries, keys, values, attention, pieces
    )
    attn_grad = grad_far(order, grad_part, *og_far, out_weight)
    query_grad, own_dk, own_dv, pair_mine, pair_sent = sparse_backward(
        core, queries, keys, values, attn_grad, attention, probs, far_k, far_v
    )

    base = [pair_mine, swap(pair_sent)]
    far = back_call(far_kernel, back, base, [8, 8], "back_far")
    r1, r3 = ring_move(far[0], 1, 1), ring_move(far[1], 1, -1)
    near = back_call(near_kernel, back, base + [r1, r3], [16, 16], "back_near")
    n1, n3 = ring_move(near[0], 1, 1), ring_move(near[1], 1, -1)

    of = out_call(out_far_kernel, order, attention, out_weight, (2,), [], [], [rows] * 2, [low, high], "out_far")
    o1, o3 = head_move(of[0], 1), head_move(of[1], -1)
    on = out_call(
        out_near_kernel, order, attention, out_weight, (1, 3), [o1, o3], [low, high], [row_count] * 2, [same] * 2, "out_near"
    )
    o1, o3 = head_move(on[0], 1), head_move(on[1], -1)
    (layer_out,) = out_call(
        out_home_kernel, order, attention, out_weight, (0,), [o1, o3], [same] * 2, [row_count], [same], "out_home"
    )

    adjoints = block_adjoints(queries, attn_grad, scale)
    own = adjoints[0] + adjoints[1]
    total = jnp.zeros_like(own)
    for step in (1, 2, 4):
        total = total + scan_step(own, total, step, True).astype(F32)
    total = after(total, pair_sent)
    total = total + scan_step(own, total, 8, True).astype(F32)
    total = total + after(scan_step(own, total, 16, True), r1, r3).astype(F32)
    later = jnp.stack([total + adjoints[1], total])
    query_grad, key_grad, value_grad = linear_backward(
        queries, keys, values, attn_grad, scale, *split(before), *split(later), query_grad
    )

    turn = back_call(turn_kernel, back, base + [after(n1, key_grad), n3], [4, 4, 2, 2, 4], "back_turn")
    home, right, far_a, far_b, left = turn
    r1, r3 = ring_move(far_a, 0, 1), ring_move(far_b, 0, -1)
    right, left = back_call(last_kernel, back, [right, left, r1, r3], [4, 4], "back_last")
    r1, r3 = ring_move(right, 0, 1), ring_move(left, 0, -1)
    mine, sent = back_call(tail_kernel, back, [home, r1, r3], [2, 2], "back_tail")
    key_grad, value_grad = finish(core, own_dk, own_dv, mine, swap(sent), key_grad, value_grad)
    return layer_out, query_grad, key_grad, value_grad


def solution(mesh):
    return jax.shard_map(
        local,
        mesh=mesh,
        in_specs=(
            P("ctx", "head"),
            P("ctx", "head"),
            P("ctx", "head"),
            P(None, "head"),
            P("ctx", "head"),
            P(),
        ),
        out_specs=(P("ctx", "head"), P("ctx", "head"), P("ctx", "head"), P("ctx", "head")),
        check_vma=False,
    )
```

```python
import functools
import math

import jax
import jax.numpy as jnp
from jax import lax
from jax.experimental import pallas as pl
from jax.experimental.pallas import tpu as pltpu
from jax.sharding import PartitionSpec as P

HD = 128
LIN = 3
LISTED = 4
BLOCK = 512
SIDE = 4
CORES = 2
CTX = SIDE * SIDE * CORES
SCALING = 1.0 / math.sqrt(HD)
BF = jnp.bfloat16
F32 = jnp.float32
MIB = 1 << 20
COSTS = 1.0
HALF = LIN * HD // CORES
UNIT = 4 * BLOCK + HALF
FRONT = 2 * BLOCK + HALF
LINE = 4 * 4 * BLOCK + 2 * HALF
MID = 8 * BLOCK
TILE = (BLOCK, HD)


def dot(a, b, ca, cb):
    return lax.dot_general(a, b, (((ca,), (cb,)), ((), ())), preferred_element_type=F32)


def params(mib):
    return pltpu.CompilerParams(vmem_limit_bytes=mib * MIB)


def cost(flops, nbytes):
    return pl.CostEstimate(flops=int(flops * COSTS), bytes_accessed=int(nbytes * COSTS), transcendentals=0)


def ring_move(value, axis, step):
    pairs = []
    for z in range(SIDE):
        for x in range(SIDE):
            for c in range(CORES):
                dx, dz = (step, 0) if axis == c else (0, step)
                to = (((z + dz) % SIDE) * SIDE + (x + dx) % SIDE) * CORES + c
                pairs.append(((z * SIDE + x) * CORES + c, to))
    return lax.ppermute(value, "ctx", pairs)


def swap(value):
    return lax.ppermute(value, "ctx", [(i, i ^ 1) for i in range(CTX)])


def copies_kernel(moves, n_in, n_deps, *refs):
    ins, outs, sems = refs[:n_in], refs[n_in + n_deps : -1], refs[-1]
    copies = [
        pltpu.make_async_copy(
            ins[i].at[pl.ds(i0, n)], outs[o].at[pl.ds(o0, n)], sems.at[m]
        )
        for m, (i, i0, o, o0, n) in enumerate(moves)
    ]
    for copy in copies:
        copy.start()
    for copy in copies:
        copy.wait()


def copies(inputs, sizes, moves, deps=()):
    anywhere = pl.BlockSpec(memory_space=pl.ANY)
    return pl.pallas_call(
        functools.partial(copies_kernel, moves, len(inputs), len(deps)),
        in_specs=[anywhere] * (len(inputs) + len(deps)),
        out_specs=[pl.BlockSpec(memory_space=pltpu.VMEM)] * len(sizes),
        out_shape=[jax.ShapeDtypeStruct((n,) + inputs[0].shape[1:], BF) for n in sizes],
        scratch_shapes=[pltpu.SemaphoreType.DMA((len(moves),))],
        compiler_params=params(16),
        cost_estimate=cost(0, sum(m[4] for m in moves) * math.prod(inputs[0].shape[1:]) * 4),
        name="copies",
    )(*inputs, *deps)


def halves(right, left, n, deps=()):
    m = left.shape[0] - n
    return copies([right, left], [n, m], [(0, 0, 0, 0, n), (1, n, 1, 0, m)], deps)


def drop(kernel, n_in, n_deps, *refs):
    kernel(*refs[:n_in], *refs[n_in + n_deps :])


ANY = pl.BlockSpec(memory_space=pl.ANY)
VM = pl.BlockSpec(memory_space=pltpu.VMEM)
SM = pl.BlockSpec(memory_space=pltpu.SMEM)


def whole_call(kernel, scalars, operands, outs, name, deps=(), scratch=(), flops=1e6):
    outs = [jax.ShapeDtypeStruct(*o) for o in outs]
    nbytes = sum(math.prod(o.shape) * o.dtype.itemsize for o in [*operands, *outs])
    n_in = len(scalars) + len(operands)
    return pl.pallas_call(
        functools.partial(drop, kernel, n_in, len(deps)),
        in_specs=[SM] * len(scalars) + [VM] * len(operands) + [ANY] * len(deps),
        out_specs=[VM] * len(outs),
        out_shape=outs,
        scratch_shapes=list(scratch),
        compiler_params=params(32),
        cost_estimate=cost(flops, nbytes),
        name=name,
    )(*scalars, *operands, *deps)


def causal_mask():
    s = lax.broadcasted_iota(jnp.int32, (BLOCK, BLOCK), 0)
    u = lax.broadcasted_iota(jnp.int32, (BLOCK, BLOCK), 1)
    return s <= u


def adjoint_kernel(q_ref, g_ref, c_ref, out_ref):
    qt = (q_ref[...].astype(F32).T * c_ref[0:1, :]).astype(BF)
    out_ref[0, 0] = dot(qt, g_ref[...], 1, 0)


def tile_spec():
    return pl.BlockSpec(TILE, lambda i, h: (i, h))


def scale_spec():
    return pl.BlockSpec((8, BLOCK), lambda i, h: (0, i))


def state_spec():
    return pl.BlockSpec((1, 1, HD, HD), lambda i, h: (i, h, 0, 0))


def block_adjoints(queries, grads, scale):
    return pl.pallas_call(
        adjoint_kernel,
        grid=(2, LIN),
        in_specs=[tile_spec(), tile_spec(), scale_spec()],
        out_specs=state_spec(),
        out_shape=jax.ShapeDtypeStruct((2, LIN, HD, HD), F32),
        compiler_params=params(16),
        cost_estimate=cost(1e8, 2 * MIB),
        name="block_adjoints",
    )(queries, grads, scale)


def split(value):
    high = value.astype(BF)
    return high, (value - high.astype(F32)).astype(BF)


def linear_forward_kernel(q_ref, k_ref, v_ref, c_ref, s_ref, out_ref):
    q, k, v, c = q_ref[...], k_ref[...], v_ref[...], c_ref[0:1, :]
    weights = jnp.where(causal_mask(), dot(k, q, 1, 1) * c, 0.0).astype(BF)
    hi, lo = split(s_ref[0, 0].T)
    out = dot(v, weights, 0, 0) + c * (dot(hi, q, 1, 1) + dot(lo, q, 1, 1))
    out_ref[...] = out.T.astype(BF)


def linear_forward(queries, keys, values, scale, before):
    return pl.pallas_call(
        linear_forward_kernel,
        grid=(2, LIN),
        in_specs=[tile_spec()] * 3 + [scale_spec(), state_spec()],
        out_specs=tile_spec(),
        out_shape=jax.ShapeDtypeStruct(queries.shape, BF),
        compiler_params=params(24),
        cost_estimate=cost(2.4e9, 4 * MIB),
        name="linear_forward",
    )(queries, keys, values, scale, before)


def linear_backward_kernel(
    q_ref, k_ref, v_ref, g_ref, c_ref, s_ref, b0, b1, b2, dep, dq_ref, dk_ref, dv_ref
):
    q, k, v, g, c = q_ref[...], k_ref[...], v_ref[...], g_ref[...], c_ref[0:1, :]
    mask = causal_mask()
    grad_weights = jnp.where(mask, dot(v, g, 1, 1) * c, 0.0).astype(BF)
    hi, lo = split(s_ref[0, 0])
    dq = dot(k, grad_weights, 0, 0) + c * (dot(hi, g, 1, 1) + dot(lo, g, 1, 1))
    dq_ref[...] = dq.T.astype(BF)
    dk_ref[...] = dot(grad_weights, q, 1, 0)
    weights = jnp.where(mask, dot(k, q, 1, 1) * c, 0.0).astype(BF)
    dv_ref[...] = dot(weights, g, 1, 0)


def linear_backward(queries, keys, values, grads, scale, before, bases, dep):
    shape = queries.shape
    return pl.pallas_call(
        linear_backward_kernel,
        grid=(2, LIN),
        in_specs=[tile_spec()] * 4 + [scale_spec(), state_spec()] + [ANY] * 4,
        out_specs=[tile_spec()] * 3,
        out_shape=[jax.ShapeDtypeStruct(shape, t) for t in (BF, F32, F32)],
        input_output_aliases={6: 0, 7: 1, 8: 2},
        compiler_params=params(24),
        cost_estimate=cost(5e9, 9 * MIB),
        name="linear_backward",
    )(queries, keys, values, grads, scale, before, *bases, dep)


def sparse_forward_kernel(table, q_ref, k_ref, v_ref, base_ref, dep, *rest):
    pieces = rest[:10]
    out_ref, p_ref, kf_ref, vf_ref, s_ref, sems = rest[10:]
    step = pl.program_id(0)
    for r in range(LISTED):
        row = step * LISTED + r
        for j in range(10):

            @pl.when(table[row, 0] == j)
            def _():
                pltpu.make_async_copy(pieces[j].at[pl.ds(pl.multiple_of(table[row, 1] * HD, HD), BLOCK)], kf_ref.at[r], sems.at[0, r]).start()

            @pl.when(table[row, 2] == j)
            def _():
                pltpu.make_async_copy(pieces[j].at[pl.ds(pl.multiple_of(table[row, 3] * HD, HD), BLOCK)], vf_ref.at[r], sems.at[1, r]).start()

    q = q_ref[...]
    s = jnp.where(causal_mask(), dot(k_ref[...], q, 1, 1) * SCALING, -1e30)
    s_ref[0] = s
    peak = jnp.max(s, axis=0, keepdims=True)
    for r in range(LISTED):
        pltpu.make_async_copy(pieces[0].at[pl.ds(0, BLOCK)], kf_ref.at[r], sems.at[0, r]).wait()
        bias = jnp.where(table[step * LISTED + r, 4] == 1, 0.0, -1e30).astype(F32)
        s = dot(kf_ref[r], q, 1, 1) * SCALING + bias
        s_ref[r + 1] = s
        peak = jnp.maximum(peak, jnp.max(s, axis=0, keepdims=True))
    total = jnp.zeros((1, BLOCK), F32)
    for r in range(LISTED + 1):
        e = jnp.exp(s_ref[r] - peak)
        s_ref[r] = e
        total = total + jnp.sum(e, axis=0, keepdims=True)
    inverse = 1.0 / total
    out = jnp.zeros((HD, BLOCK), F32)
    for r in range(LISTED + 1):
        p = (s_ref[r] * inverse).astype(BF)
        p_ref[0, r] = p
        if r == 0:
            value = v_ref[...]
        else:
            pltpu.make_async_copy(pieces[0].at[pl.ds(0, BLOCK)], vf_ref.at[r - 1], sems.at[1, r - 1]).wait()
            value = vf_ref[r - 1]
        out = out + dot(value, p, 0, 0)
    out_ref[...] = out.T.astype(BF)


def sparse_forward(table, queries, keys, values, base, dep, pieces):
    column = pl.BlockSpec(TILE, lambda i, t: (i, LIN))
    anywhere = pl.BlockSpec(memory_space=pl.ANY)
    return pl.pallas_call(
        sparse_forward_kernel,
        grid_spec=pltpu.PrefetchScalarGridSpec(
            num_scalar_prefetch=1,
            grid=(2,),
            in_specs=[column] * 3 + [anywhere] * 12,
            out_specs=[
                column,
                pl.BlockSpec((1, LISTED + 1, BLOCK, BLOCK), lambda i, t: (i, 0, 0, 0)),
                pl.BlockSpec((LISTED, BLOCK, HD), lambda i, t: (i, 0, 0)),
                pl.BlockSpec((LISTED, BLOCK, HD), lambda i, t: (i, 0, 0)),
            ],
            scratch_shapes=[
                pltpu.VMEM((LISTED + 1, BLOCK, BLOCK), F32),
                pltpu.SemaphoreType.DMA((2, LISTED)),
            ],
        ),
        out_shape=[
            jax.ShapeDtypeStruct(queries.shape, BF),
            jax.ShapeDtypeStruct((2, LISTED + 1, BLOCK, BLOCK), BF),
            jax.ShapeDtypeStruct((2 * LISTED, BLOCK, HD), BF),
            jax.ShapeDtypeStruct((2 * LISTED, BLOCK, HD), BF),
        ],
        input_output_aliases={4: 0},
        compiler_params=params(32),
        cost_estimate=cost(4e9, 12 * MIB),
        name="sparse_forward",
    )(table, queries, keys, values, base, dep, *pieces)


def sparse_backward_kernel(
    core, q_ref, k_ref, v_ref, g_ref, o_ref, p_ref, kf_ref, vf_ref, dep, dq_ref, dk_ref, dv_ref, mine_ref, sent_ref
):
    first = core[0] == 0
    q, g = q_ref[...], g_ref[...]
    row_dot = jnp.sum((g.astype(F32) * o_ref[...].astype(F32)).T, axis=0, keepdims=True)
    dq = jnp.zeros((HD, BLOCK), F32)
    for r in range(LISTED + 1):
        p = p_ref[0, r]
        key = k_ref[...] if r == 0 else kf_ref[r - 1]
        value = v_ref[...] if r == 0 else vf_ref[r - 1]
        dp = dot(value, g, 1, 1)
        ds = (p.astype(F32) * (dp - row_dot)).astype(BF)
        dq = dq + dot(key, ds, 0, 0)
        dk = dot(ds, q, 1, 0) * SCALING
        dv = dot(p, g, 1, 0)
        if r == 0:
            dk_ref[...] = dk
            dv_ref[...] = dv
        else:
            mine_ref[r - 1] = jnp.where(first, dk, dv).astype(BF)
            sent_ref[r - 1] = jnp.where(first, dv, dk).astype(BF)
    dq_ref[...] = (dq * SCALING).T.astype(BF)


def sparse_backward(core, queries, keys, values, grads, outs, probs, far_k, far_v, dep):
    column = pl.BlockSpec(TILE, lambda i, c: (i, LIN))
    four = pl.BlockSpec((LISTED, BLOCK, HD), lambda i, c: (i, 0, 0))
    five = pl.BlockSpec((1, LISTED + 1, BLOCK, BLOCK), lambda i, c: (i, 0, 0, 0))
    return pl.pallas_call(
        sparse_backward_kernel,
        grid_spec=pltpu.PrefetchScalarGridSpec(
            num_scalar_prefetch=1,
            grid=(2,),
            in_specs=[column] * 3
            + [pl.BlockSpec(TILE, lambda i, c: (i, 0)), column, five, four, four, ANY],
            out_specs=[column, column, column, four, four],
        ),
        out_shape=[
            jax.ShapeDtypeStruct(queries.shape, BF),
            jax.ShapeDtypeStruct(queries.shape, F32),
            jax.ShapeDtypeStruct(queries.shape, F32),
            jax.ShapeDtypeStruct((2 * LISTED, BLOCK, HD), BF),
            jax.ShapeDtypeStruct((2 * LISTED, BLOCK, HD), BF),
        ],
        compiler_params=params(32),
        cost_estimate=cost(8e9, 12 * MIB),
        name="sparse_backward",
    )(core, queries, keys, values, grads, outs, probs, far_k, far_v, dep)


def begin_kernel(core, k_ref, v_ref, states, mine, sent):
    first = core[0] == 0
    for h in range(LIN):
        at = pl.ds(h * HD, HD)
        s0 = dot(k_ref[0:BLOCK, at], v_ref[0:BLOCK, at], 0, 0)
        s1 = dot(k_ref[BLOCK:, at], v_ref[BLOCK:, at], 0, 0)
        states[0, h] = s0
        states[1, h] = s1
        sent[2 * BLOCK + h * HD : 2 * BLOCK + (h + 1) * HD] = (s0 + s1).astype(BF)
    at = pl.ds(LIN * HD, HD)
    k, v = k_ref[:, at], v_ref[:, at]
    mine[...] = jnp.where(first, k, v)
    sent[0 : 2 * BLOCK] = jnp.where(first, v, k)


def start_kernel(core, mine, got, states, out, scratch):
    out[0 : 2 * BLOCK] = mine[...]
    out[FRONT:] = got[0 : 2 * BLOCK]
    for h in range(LIN):
        other = got[2 * BLOCK + h * HD : 2 * BLOCK + (h + 1) * HD].astype(F32)
        scratch[h * HD : (h + 1) * HD] = states[0, h] + states[1, h] + other
    out[2 * BLOCK : FRONT] = scratch[pl.ds(pl.multiple_of(core[0] * HALF, HALF), HALF)].astype(BF)


def line_kernel(core, earlier, start, right, far_a, far_b, left, line, local):
    for spot, piece in ((0, start), (4 * BLOCK, right), (MID + 2 * HALF + 4 * BLOCK, left)):
        line[spot : spot + 2 * BLOCK] = piece[0 : 2 * BLOCK]
        line[spot + 2 * BLOCK : spot + 4 * BLOCK] = piece[FRONT:]
    spot = MID + 2 * HALF
    line[spot : spot + 2 * BLOCK] = far_a[0 : 2 * BLOCK]
    line[spot + 2 * BLOCK : spot + 4 * BLOCK] = far_b[...]
    first = core[0] == 0
    s = [p[2 * BLOCK : FRONT].astype(F32) for p in (start, right, far_a, left)]
    m = [earlier[0, p].astype(F32) for p in range(SIDE)]
    before = s[1] * m[1] + s[2] * m[2] + s[3] * m[3]
    total = s[0] + s[1] + s[2] + s[3]
    line[MID : MID + HALF] = jnp.where(first, total, s[0]).astype(BF)
    line[MID + HALF : MID + 2 * HALF] = jnp.where(first, 0.0, before).astype(BF)
    local[...] = before


def prefix_kernel(earlier, local, right, far, left, out, scratch, sems):
    got = [
        pltpu.make_async_copy(piece.at[pl.ds(MID, 2 * HALF)], scratch.at[n], sems.at[n])
        for n, piece in enumerate((right, far, left))
    ]
    for copy in got:
        copy.start()
    for copy in got:
        copy.wait()
    total = local[...]
    for n in range(3):
        total = total + scratch[n, 0:HALF].astype(F32) * earlier[1, n + 1].astype(F32)
        total = total + scratch[n, HALF:].astype(F32)
    out[...] = total


def prefix(earlier, local, right, far, left):
    return pl.pallas_call(
        prefix_kernel,
        in_specs=[SM, VM, ANY, ANY, ANY],
        out_specs=VM,
        out_shape=jax.ShapeDtypeStruct((HALF, HD), F32),
        scratch_shapes=[pltpu.VMEM((3, 2 * HALF, HD), BF), pltpu.SemaphoreType.DMA((3,))],
        compiler_params=params(4),
        cost_estimate=cost(1e5, MIB // 2),
        name="prefix",
    )(earlier, local, right, far, left)


SPOTS = (0, BLOCK, FRONT, FRONT + BLOCK)


def placed(table, j, own_ref, peer_ref):
    a, b = table[0, j], table[1, j]
    first = own_ref[jnp.maximum(a, 0)].astype(F32) * jnp.where(a >= 0, 1.0, 0.0).astype(F32)
    second = peer_ref[jnp.maximum(b, 0)].astype(F32) * jnp.where(b >= 0, 1.0, 0.0).astype(F32)
    return first + second


def fill(table, own, peer, half, j, out, u, more=(), m=0):
    for q, spot in enumerate(SPOTS):
        at = pl.ds(spot, BLOCK)
        value = placed(table, 4 * j + q, own, peer)
        for ref in more:
            value = value + ref[m, at].astype(F32)
        out[u, at] = value.astype(BF)
    at = pl.ds(2 * BLOCK, HALF)
    value = half[...] * table[2, j].astype(F32)
    for ref in more:
        value = value + ref[m, at].astype(F32)
    out[u, at] = value.astype(BF)


def far_kernel(table, own, peer, half, far_a, far_b):
    @pl.loop(0, 2)
    def _(u):
        fill(table, own, peer, half, 8 + u, far_a, u)
        fill(table, own, peer, half, 10 + u, far_b, u)


def near_kernel(table, own, peer, half, ra, rb, right, left):
    @pl.loop(0, 2)
    def _(u):
        fill(table, own, peer, half, 4 + u, right, u, [ra], u)
        fill(table, own, peer, half, 6 + u, right, u + 2)
        fill(table, own, peer, half, 12 + u, left, u)
        fill(table, own, peer, half, 14 + u, left, u + 2, [rb], u)


def turn_kernel(table, own, peer, half, r1, r3, home, right, far_a, far_b, left, unit):
    @pl.loop(0, SIDE)
    def _(u):
        fill(table, own, peer, half, u, unit, u, [r1, r3], u)

    home[...] = unit[0]
    right[...] = unit[1]
    far_a[...] = unit[2, 0:FRONT]
    far_b[...] = unit[2, FRONT:]
    left[...] = unit[3]


def last_kernel(right, left, ra, rb, o_right, o_left):
    o_right[0:FRONT] = (right[0:FRONT].astype(F32) + ra[...].astype(F32)).astype(BF)
    o_right[FRONT:] = right[FRONT:]
    o_left[0:FRONT] = left[0:FRONT]
    o_left[FRONT:] = (left[FRONT:].astype(F32) + rb[...].astype(F32)).astype(BF)


def tail_kernel(home, r1, r3, mine, sent, extra):
    def total(a, b):
        return home[a:b].astype(F32) + r1[a:b].astype(F32) + r3[a:b].astype(F32)

    mine[...] = total(0, 2 * BLOCK).astype(BF)
    more = total(2 * BLOCK, FRONT)
    extra[...] = more
    sent[0 : 2 * BLOCK] = total(FRONT, UNIT).astype(BF)
    sent[2 * BLOCK :] = more.astype(BF)


def finish_kernel(core, k_ref, v_ref, dk, dv, mine_ref, got_ref, tail_ref, extra, adj, peer, kg, vg, scratch):
    first = core[0] == 0
    mine, got = mine_ref[...].astype(F32), got_ref[...].astype(F32)
    at = pl.ds(LIN * HD, HD)
    kg[:, at] = (dk[:, at] + jnp.where(first, mine, got)).astype(BF)
    vg[:, at] = (dv[:, at] + jnp.where(first, got, mine)).astype(BF)
    tail = tail_ref[...].astype(F32)
    scratch[0:HALF] = jnp.where(first, extra[...], tail)
    scratch[HALF:] = jnp.where(first, tail, extra[...])
    inner = jnp.where(pl.program_id(0) == 0, 1.0, 0.0).astype(F32)
    chip = jnp.where(first, 1.0, 0.0).astype(F32)
    for h in range(LIN):
        at = pl.ds(h * HD, HD)
        state = scratch[at, :] + peer[at, :].astype(F32) * chip + adj[1, h] * inner
        hi, lo = split(state)
        k, v = k_ref[:, at], v_ref[:, at]
        kg[:, at] = (dk[:, at] + dot(v, hi, 1, 1) + dot(v, lo, 1, 1)).astype(BF)
        vg[:, at] = (dv[:, at] + dot(k, hi, 1, 0) + dot(k, lo, 1, 0)).astype(BF)


def finish(core, keys, values, dk, dv, mine, got, extra, adjoints, peer):
    rows = pl.BlockSpec((BLOCK, keys.shape[1]), lambda i, c: (i, 0))
    piece = pl.BlockSpec((BLOCK, HD), lambda i, c: (i, 0))
    fixed = [
        pl.BlockSpec((HALF, HD), lambda i, c: (0, 0)),
        pl.BlockSpec(adjoints.shape, lambda i, c: (0, 0, 0, 0)),
        pl.BlockSpec((LIN * HD, HD), lambda i, c: (0, 0)),
    ]
    shape = jax.ShapeDtypeStruct(keys.shape, BF)
    return pl.pallas_call(
        finish_kernel,
        grid_spec=pltpu.PrefetchScalarGridSpec(
            num_scalar_prefetch=1,
            grid=(2,),
            in_specs=[rows] * 4 + [piece, piece, fixed[0]] + fixed,
            out_specs=[rows, rows],
            scratch_shapes=[pltpu.VMEM((LIN * HD, HD), F32)],
        ),
        out_shape=[shape, shape],
        compiler_params=params(32),
        cost_estimate=cost(5e8, 9 * MIB),
        name="finish",
    )(core, keys, values, dk, dv, mine, got, got[2 * BLOCK :], extra, adjoints, peer)


def where_is(blocks, place):
    owner, within = blocks // 2, blocks % 2
    pz = (place // (SIDE * CORES) - owner // (SIDE * CORES)) % SIDE
    px = (place // CORES % SIDE - owner // CORES % SIDE) % SIDE
    return pz, px, owner % CORES, within


def spot_of(blocks, place, stream):
    pz, px, core, within = where_is(blocks, place)
    rel = (core != stream).astype(jnp.int32)
    outer = jnp.where(stream == 0, pz, px)
    first = jnp.where(stream == 0, px, pz)
    return outer, first, rel * 2 + within


def spot_of(blocks, place, stream):
    pz, px, core, within = where_is(blocks, place)
    rel = (core != stream).astype(jnp.int32)
    outer = jnp.where(stream == 0, pz, px)
    first = jnp.where(stream == 0, px, pz)
    return outer, first, rel * 2 + within


def piece_of(blocks, place, stream):
    outer, first, rest = spot_of(blocks, place, stream)
    late = first >= 2
    second = (outer == 2) & late
    piece = jnp.where(outer < 2, outer, jnp.where(outer == 3, 4, jnp.where(second, 3, 2)))
    index = first * 16 + rest * 4 + jnp.where(late, 3, 0) - jnp.where(second, 35, 0)
    return piece + 5 * (place % CORES != stream).astype(jnp.int32), index


def fetch_table(lists, place):
    flat = lists.reshape(-1)
    mine = place * 2 + jnp.arange(2 * LISTED, dtype=jnp.int32) // LISTED
    usable = (flat != mine).astype(jnp.int32)
    columns = [*piece_of(flat, place, 0), *piece_of(flat, place, 1), usable]
    return jnp.stack(columns, axis=1).astype(jnp.int32)


def back_table(lists, peer_lists, place):
    slots = jnp.arange(2 * LISTED, dtype=jnp.int32)[:, None]
    spots = jnp.arange(64, dtype=jnp.int32)[None, :]
    rows = []
    for some in (lists, peer_lists):
        outer, first, rest = spot_of(some.reshape(-1), place, place % CORES)
        target = (-outer) % SIDE * 16 + (-first) % SIDE * 4 + rest
        rows.append(jnp.max(jnp.where(target[:, None] == spots, slots, -1), axis=0))
    z, x = place // (SIDE * CORES), place // CORES % SIDE
    step = jnp.arange(64, dtype=jnp.int32)
    outer, inner = step // SIDE, step % SIDE
    on_keys = place % CORES == 0
    to_z = (z + jnp.where(on_keys, outer, inner)) % SIDE
    to_x = (x + jnp.where(on_keys, inner, outer)) % SIDE
    rows.append((to_z * SIDE + to_x < z * SIDE + x).astype(jnp.int32))
    return jnp.stack(rows).astype(jnp.int32)


def earlier_table(place):
    z, x = place // (SIDE * CORES), place // CORES % SIDE
    on_keys = place % CORES == 0
    first, second = jnp.where(on_keys, x, z), jnp.where(on_keys, z, x)
    step = jnp.arange(SIDE, dtype=jnp.int32)
    rows = [(c - step) % SIDE < c for c in (first, second)]
    return jnp.stack(rows).astype(jnp.int32)


def local(queries, keys, values, out_weight, out_grad, long_blocks):
    place = lax.axis_index("ctx").astype(jnp.int32)
    core = (place % CORES).reshape(1)
    row_count = queries.shape[0]
    positions = place * row_count + jnp.arange(row_count, dtype=jnp.int32)
    scale = 1.0 / (math.sqrt(HD) * jnp.sqrt((positions + 1).astype(F32)))
    scale = jnp.broadcast_to(scale[None, :], (8, row_count))
    lists = lax.dynamic_slice_in_dim(long_blocks, place * 2, 2, 0)
    peer_lists = lax.dynamic_slice_in_dim(long_blocks, (place ^ 1) * 2, 2, 0)
    fetch = fetch_table(lists, place)
    back = back_table(lists, peer_lists, place)
    earlier = earlier_table(place)

    grad_all = lax.all_gather(out_grad, "head", axis=1, tiled=True)

    states, mine, sent = whole_call(
        begin_kernel,
        [core],
        [keys, values],
        [((2, LIN, HD, HD), F32), ((2 * BLOCK, HD), BF), ((2 * BLOCK + LIN * HD, HD), BF)],
        "begin",
    )
    got = swap(sent)
    (start,) = whole_call(
        start_kernel, [core], [mine, got, states], [((UNIT, HD), BF)], "start",
        scratch=[pltpu.VMEM((LIN * HD, HD), F32)],
    )
    a_right, a_left = ring_move(start, 0, 1), ring_move(start, 0, -1)
    cut = halves(a_right, a_left, FRONT)
    a_far = ring_move(cut[0], 0, 1), ring_move(cut[1], 0, -1)
    line, inside = whole_call(
        line_kernel, [core, earlier], [start, a_right, *a_far, a_left],
        [((LINE, HD), BF), ((HALF, HD), F32)], "line",
    )
    b_right, b_left = ring_move(line, 1, 1), ring_move(line, 1, -1)
    line_swapped = swap(line)
    cut = halves(b_right, b_left, MID + 2 * HALF, [line_swapped])
    b_far = ring_move(cut[0], 1, 1), ring_move(cut[1], 1, -1)
    pieces = [line, b_right, *b_far, b_left]
    pieces = pieces + [line_swapped] + [swap(p) for p in pieces[1:]]
    part = prefix(earlier, inside, b_right, b_far[0], b_left)
    other = swap(part)
    on_keys = place % CORES == 0
    chip = jnp.where(on_keys, jnp.concatenate([part, other]), jnp.concatenate([other, part]))
    chip = chip + jnp.where(on_keys, 0.0, got[2 * BLOCK :].astype(F32))
    chip = chip.reshape(LIN, HD, HD)
    before = jnp.stack([chip, chip + states[0]])

    attention = linear_forward(queries, keys, values, scale, before)
    attention, probs, far_k, far_v = sparse_forward(
        fetch, queries, keys, values, attention, inside, pieces
    )
    partial_out = dot(attention, out_weight, 1, 1).astype(BF)
    layer_out = lax.psum_scatter(partial_out, "head", scatter_dimension=1, tiled=True)
    sparse_grad = dot(grad_all, out_weight[:, LIN * HD :], 1, 0).astype(BF)
    linear_grad = dot(grad_all, out_weight[:, : LIN * HD], 1, 0).astype(BF)
    query_grad, own_dk, own_dv, pair_mine, pair_sent = sparse_backward(
        core, queries, keys, values, sparse_grad, attention, probs, far_k, far_v, inside
    )

    adjoints = block_adjoints(queries, linear_grad, scale)
    adjoint = (adjoints[0] + adjoints[1]).reshape(LIN * HD, HD)
    adjoint_peer = swap(adjoint.astype(BF))
    half = lax.dynamic_slice_in_dim(
        adjoint + adjoint_peer.astype(F32), place % CORES * HALF, HALF, 0
    )
    base = [pair_mine, swap(pair_sent), half]
    far_a, far_b = whole_call(
        far_kernel, [back], base, [((2, UNIT, HD), BF)] * 2, "back_far"
    )
    r1, r3 = ring_move(far_a, 1, 1), ring_move(far_b, 1, -1)
    near = whole_call(
        near_kernel, [back], base + [r1, r3], [((SIDE, UNIT, HD), BF)] * 2, "back_near"
    )
    r1, r3 = ring_move(near[0], 1, 1), ring_move(near[1], 1, -1)

    query_grad, own_dk, own_dv = linear_backward(
        queries, keys, values, linear_grad, scale, before, (query_grad, own_dk, own_dv), inside
    )

    home, right, far_a, far_b, left = whole_call(
        turn_kernel, [back], base + [r1, r3],
        [((UNIT, HD), BF), ((UNIT, HD), BF), ((FRONT, HD), BF), ((2 * BLOCK, HD), BF), ((UNIT, HD), BF)],
        "back_turn", deps=[query_grad], scratch=[pltpu.VMEM((SIDE, UNIT, HD), BF)],
    )
    r1, r3 = ring_move(far_a, 0, 1), ring_move(far_b, 0, -1)
    right, left = whole_call(
        last_kernel, [], [right, left, r1, r3], [((UNIT, HD), BF)] * 2, "back_last"
    )
    r1, r3 = ring_move(right, 0, 1), ring_move(left, 0, -1)
    mine, sent, extra = whole_call(
        tail_kernel, [], [home, r1, r3],
        [((2 * BLOCK, HD), BF), ((FRONT, HD), BF), ((HALF, HD), F32)], "back_tail",
    )
    key_grad, value_grad = finish(
        core, keys, values, own_dk, own_dv, mine, swap(sent), extra, adjoints, adjoint_peer
    )
    return layer_out, query_grad, key_grad, value_grad


def solution(mesh):
    return jax.shard_map(
        local,
        mesh=mesh,
        in_specs=(
            P("ctx", "head"),
            P("ctx", "head"),
            P("ctx", "head"),
            P(None, "head"),
            P("ctx", "head"),
            P(),
        ),
        out_specs=(P("ctx", "head"), P("ctx", "head"), P("ctx", "head"), P("ctx", "head")),
        check_vma=False,
    )
```

```python
import functools
import math

import jax
import jax.numpy as jnp
from jax import lax
from jax.experimental import pallas as pl
from jax.experimental.pallas import tpu as pltpu
from jax.sharding import PartitionSpec as P

HD = 128
LIN = 3
LISTED = 4
BLOCK = 512
SIDE = 4
CORES = 2
CTX = SIDE * SIDE * CORES
SCALING = 1.0 / math.sqrt(HD)
BF = jnp.bfloat16
F32 = jnp.float32
MIB = 1 << 20
COSTS = 1.0
HALF = LIN * HD // CORES
UNIT = 4 * BLOCK + HALF
FRONT = 2 * BLOCK + HALF
MID = 8 * BLOCK
TILE = (BLOCK, HD)


def dot(a, b, ca, cb):
    return lax.dot_general(a, b, (((ca,), (cb,)), ((), ())), preferred_element_type=F32)


def params(mib):
    return pltpu.CompilerParams(vmem_limit_bytes=mib * MIB)


def cost(flops, nbytes):
    return pl.CostEstimate(flops=int(flops * COSTS), bytes_accessed=int(nbytes * COSTS), transcendentals=0)


def ring_move(value, axis, step):
    pairs = []
    for z in range(SIDE):
        for x in range(SIDE):
            for c in range(CORES):
                dx, dz = (step, 0) if axis == c else (0, step)
                to = (((z + dz) % SIDE) * SIDE + (x + dx) % SIDE) * CORES + c
                pairs.append(((z * SIDE + x) * CORES + c, to))
    return lax.ppermute(value, "ctx", pairs)


def swap(value):
    return lax.ppermute(value, "ctx", [(i, i ^ 1) for i in range(CTX)])


def drop(kernel, n_in, n_deps, *refs):
    kernel(*refs[:n_in], *refs[n_in + n_deps :])


ANY = pl.BlockSpec(memory_space=pl.ANY)
VM = pl.BlockSpec(memory_space=pltpu.VMEM)
SM = pl.BlockSpec(memory_space=pltpu.SMEM)


def whole_call(kernel, scalars, operands, outs, name, deps=(), scratch=(), flops=1e6):
    outs = [jax.ShapeDtypeStruct(*o) for o in outs]
    nbytes = sum(math.prod(o.shape) * o.dtype.itemsize for o in [*operands, *outs])
    n_in = len(scalars) + len(operands)
    return pl.pallas_call(
        functools.partial(drop, kernel, n_in, len(deps)),
        in_specs=[SM] * len(scalars) + [VM] * len(operands) + [ANY] * len(deps),
        out_specs=[VM] * len(outs),
        out_shape=outs,
        scratch_shapes=list(scratch),
        compiler_params=params(32),
        cost_estimate=cost(flops, nbytes),
        name=name,
    )(*scalars, *operands, *deps)


def causal_mask():
    s = lax.broadcasted_iota(jnp.int32, (BLOCK, BLOCK), 0)
    u = lax.broadcasted_iota(jnp.int32, (BLOCK, BLOCK), 1)
    return s <= u


def adjoint_kernel(q_ref, g_ref, c_ref, out_ref):
    qt = (q_ref[...].astype(F32).T * c_ref[0:1, :]).astype(BF)
    out_ref[0, 0] = dot(qt, g_ref[...], 1, 0)


def tile_spec():
    return pl.BlockSpec(TILE, lambda i, h: (i, h))


def scale_spec():
    return pl.BlockSpec((8, BLOCK), lambda i, h: (0, i))


def state_spec():
    return pl.BlockSpec((1, 1, HD, HD), lambda i, h: (i, h, 0, 0))


def block_adjoints(queries, grads, scale):
    return pl.pallas_call(
        adjoint_kernel,
        grid=(2, LIN),
        in_specs=[tile_spec(), tile_spec(), scale_spec()],
        out_specs=state_spec(),
        out_shape=jax.ShapeDtypeStruct((2, LIN, HD, HD), F32),
        compiler_params=params(16),
        cost_estimate=cost(1e8, 2 * MIB),
        name="block_adjoints",
    )(queries, grads, scale)


def split(value):
    high = value.astype(BF)
    return high, (value - high.astype(F32)).astype(BF)


def linear_forward_kernel(q_ref, k_ref, v_ref, c_ref, s_ref, base_ref, out_ref):
    q, k, v, c = q_ref[...], k_ref[...], v_ref[...], c_ref[0:1, :]
    weights = jnp.where(causal_mask(), dot(k, q, 1, 1) * c, 0.0).astype(BF)
    hi, lo = split(s_ref[0, 0].T)
    out = dot(v, weights, 0, 0) + c * (dot(hi, q, 1, 1) + dot(lo, q, 1, 1))
    out_ref[...] = out.T.astype(BF)


def linear_forward(queries, keys, values, scale, before, base):
    return pl.pallas_call(
        linear_forward_kernel,
        grid=(2, LIN),
        in_specs=[tile_spec()] * 3 + [scale_spec(), state_spec(), ANY],
        out_specs=tile_spec(),
        out_shape=jax.ShapeDtypeStruct(queries.shape, BF),
        input_output_aliases={5: 0},
        compiler_params=params(12),
        cost_estimate=cost(2.4e9, 4 * MIB),
        name="linear_forward",
    )(queries, keys, values, scale, before, base)


def linear_backward_kernel(
    q_ref, k_ref, v_ref, g_ref, c_ref, s_ref, b0, b1, b2, dep, dq_ref, dk_ref, dv_ref
):
    q, k, v, g, c = q_ref[...], k_ref[...], v_ref[...], g_ref[...], c_ref[0:1, :]
    mask = causal_mask()
    grad_weights = jnp.where(mask, dot(v, g, 1, 1) * c, 0.0).astype(BF)
    hi, lo = split(s_ref[0, 0])
    dq = dot(k, grad_weights, 0, 0) + c * (dot(hi, g, 1, 1) + dot(lo, g, 1, 1))
    dq_ref[...] = dq.T.astype(BF)
    dk_ref[...] = dot(grad_weights, q, 1, 0)
    weights = jnp.where(mask, dot(k, q, 1, 1) * c, 0.0).astype(BF)
    dv_ref[...] = dot(weights, g, 1, 0)


def linear_backward(queries, keys, values, grads, scale, before, bases, dep):
    shape = queries.shape
    return pl.pallas_call(
        linear_backward_kernel,
        grid=(2, LIN),
        in_specs=[tile_spec()] * 4 + [scale_spec(), state_spec()] + [ANY] * 4,
        out_specs=[tile_spec()] * 3,
        out_shape=[jax.ShapeDtypeStruct(shape, t) for t in (BF, F32, F32)],
        input_output_aliases={6: 0, 7: 1, 8: 2},
        compiler_params=params(16),
        cost_estimate=cost(5e9, 9 * MIB),
        name="linear_backward",
    )(queries, keys, values, grads, scale, before, *bases, dep)


PIECES = 16


def sparse_forward_kernel(table, q_ref, k_ref, v_ref, *rest):
    pieces = rest[:PIECES]
    out_ref, p_ref, kf_ref, vf_ref, inv_ref, s_ref, sems = rest[PIECES:]
    step = pl.program_id(0)

    @pl.when(step == 0)
    def _():
        @pl.loop(0, 2 * LISTED)
        def _(row):
            for j in range(PIECES):
                for n, far in ((0, kf_ref), (1, vf_ref)):

                    @pl.when(table[row, 2 * n] == j)
                    def _():
                        at = pl.ds(pl.multiple_of(table[row, 2 * n + 1] * HD, HD), BLOCK)
                        pltpu.make_async_copy(pieces[j].at[at], far.at[row], sems.at[n, row]).start()

    q = q_ref[...]
    s = jnp.where(causal_mask(), dot(k_ref[...], q, 1, 1) * SCALING, -1e30)
    s_ref[0] = s
    peak = jnp.max(s, axis=0, keepdims=True)
    for r in range(LISTED):
        row = step * LISTED + r
        pltpu.make_async_copy(pieces[0].at[pl.ds(0, BLOCK)], kf_ref.at[row], sems.at[0, row]).wait()
        bias = jnp.where(table[row, 4] == 1, 0.0, -1e30).astype(F32)
        s = dot(kf_ref[row], q, 1, 1) * SCALING + bias
        s_ref[r + 1] = s
        peak = jnp.maximum(peak, jnp.max(s, axis=0, keepdims=True))
    total = jnp.zeros((1, BLOCK), F32)
    out = jnp.zeros((HD, BLOCK), F32)
    for r in range(LISTED + 1):
        e = jnp.exp(s_ref[r] - peak)
        total = total + jnp.sum(e, axis=0, keepdims=True)
        p = e.astype(BF)
        p_ref[0, r] = p
        if r == 0:
            value = v_ref[...]
        else:
            row = step * LISTED + r - 1
            pltpu.make_async_copy(pieces[0].at[pl.ds(0, BLOCK)], vf_ref.at[row], sems.at[1, row]).wait()
            value = vf_ref[row]
        out = out + dot(value, p, 0, 0)
    inverse = 1.0 / total
    inv_ref[...] = jnp.broadcast_to(inverse, (8, BLOCK))
    out_ref[...] = (out * inverse).T.astype(BF)


def sparse_forward(table, queries, keys, values, pieces):
    column = pl.BlockSpec(TILE, lambda i, t: (i, LIN))
    far = (2 * LISTED, BLOCK, HD)
    return pl.pallas_call(
        sparse_forward_kernel,
        grid_spec=pltpu.PrefetchScalarGridSpec(
            num_scalar_prefetch=1,
            grid=(2,),
            in_specs=[column] * 3 + [ANY] * PIECES,
            out_specs=[
                column,
                pl.BlockSpec((1, LISTED + 1, BLOCK, BLOCK), lambda i, t: (i, 0, 0, 0)),
                pl.BlockSpec(far, lambda i, t: (0, 0, 0)),
                pl.BlockSpec(far, lambda i, t: (0, 0, 0)),
                pl.BlockSpec((8, BLOCK), lambda i, t: (0, i)),
            ],
            scratch_shapes=[
                pltpu.VMEM((LISTED + 1, BLOCK, BLOCK), F32),
                pltpu.SemaphoreType.DMA((2, 2 * LISTED)),
            ],
        ),
        out_shape=[
            jax.ShapeDtypeStruct(queries.shape, BF),
            jax.ShapeDtypeStruct((2, LISTED + 1, BLOCK, BLOCK), BF),
            jax.ShapeDtypeStruct(far, BF),
            jax.ShapeDtypeStruct(far, BF),
            jax.ShapeDtypeStruct((8, queries.shape[0]), F32),
        ],
        compiler_params=params(20),
        cost_estimate=cost(4e9, 12 * MIB),
        name="sparse_forward",
    )(table, queries, keys, values, *pieces)


def sparse_backward_kernel(
    core, q_ref, k_ref, v_ref, g_ref, o_ref, p_ref, kf_ref, vf_ref, inv_ref, dq_ref, dk_ref, dv_ref, mine_ref, sent_ref
):
    first = core[0] == 0
    q, g = q_ref[...], g_ref[...]
    inverse = inv_ref[0:1, :]
    turned = g.astype(F32).T * inverse
    row_dot = jnp.sum(turned * o_ref[...].astype(F32).T, axis=0, keepdims=True)
    g = turned.T.astype(BF)
    dq = jnp.zeros((HD, BLOCK), F32)
    for r in range(LISTED + 1):
        p = p_ref[0, r]
        key = k_ref[...] if r == 0 else kf_ref[r - 1]
        value = v_ref[...] if r == 0 else vf_ref[r - 1]
        dp = dot(value, g, 1, 1)
        ds = (p.astype(F32) * (dp - row_dot)).astype(BF)
        dq = dq + dot(key, ds, 0, 0)
        dk = dot(ds, q, 1, 0) * SCALING
        dv = dot(p, g, 1, 0)
        if r == 0:
            dk_ref[...] = dk
            dv_ref[...] = dv
        else:
            mine_ref[r - 1] = jnp.where(first, dk, dv).astype(BF)
            sent_ref[r - 1] = jnp.where(first, dv, dk).astype(BF)
    dq_ref[...] = (dq * SCALING).T.astype(BF)


def sparse_backward(core, queries, keys, values, grads, outs, probs, far_k, far_v, inverse):
    column = pl.BlockSpec(TILE, lambda i, c: (i, LIN))
    four = pl.BlockSpec((LISTED, BLOCK, HD), lambda i, c: (i, 0, 0))
    five = pl.BlockSpec((1, LISTED + 1, BLOCK, BLOCK), lambda i, c: (i, 0, 0, 0))
    return pl.pallas_call(
        sparse_backward_kernel,
        grid_spec=pltpu.PrefetchScalarGridSpec(
            num_scalar_prefetch=1,
            grid=(2,),
            in_specs=[column] * 3
            + [pl.BlockSpec(TILE, lambda i, c: (i, 0)), column, five, four, four]
            + [pl.BlockSpec((8, BLOCK), lambda i, c: (0, i))],
            out_specs=[column, column, column, four, four],
        ),
        out_shape=[
            jax.ShapeDtypeStruct(queries.shape, BF),
            jax.ShapeDtypeStruct(queries.shape, F32),
            jax.ShapeDtypeStruct(queries.shape, F32),
            jax.ShapeDtypeStruct((2 * LISTED, BLOCK, HD), BF),
            jax.ShapeDtypeStruct((2 * LISTED, BLOCK, HD), BF),
        ],
        compiler_params=params(20),
        cost_estimate=cost(8e9, 12 * MIB),
        name="sparse_backward",
    )(core, queries, keys, values, grads, outs, probs, far_k, far_v, inverse)


def begin_kernel(core, k_ref, v_ref, states, mine, sent):
    first = core[0] == 0
    for h in range(LIN):
        at = pl.ds(h * HD, HD)
        s0 = dot(k_ref[0:BLOCK, at], v_ref[0:BLOCK, at], 0, 0)
        s1 = dot(k_ref[BLOCK:, at], v_ref[BLOCK:, at], 0, 0)
        states[0, h] = s0
        states[1, h] = s1
        sent[2 * BLOCK + h * HD : 2 * BLOCK + (h + 1) * HD] = (s0 + s1).astype(BF)
    at = pl.ds(LIN * HD, HD)
    k, v = k_ref[:, at], v_ref[:, at]
    mine[...] = jnp.where(first, k, v)
    sent[0 : 2 * BLOCK] = jnp.where(first, v, k)


def start_kernel(core, mine, got, states, out, rest, scratch):
    out[0 : 2 * BLOCK] = mine[...]
    rest[...] = got[0 : 2 * BLOCK]
    for h in range(LIN):
        other = got[2 * BLOCK + h * HD : 2 * BLOCK + (h + 1) * HD].astype(F32)
        scratch[h * HD : (h + 1) * HD] = states[0, h] + states[1, h] + other
    out[2 * BLOCK : FRONT] = scratch[pl.ds(pl.multiple_of(core[0] * HALF, HALF), HALF)].astype(BF)


def line_kernel(core, earlier, sa, sb, ra, rb, fa, fb, la, lb, low, line, local):
    for n, (one, two) in enumerate(((sa, fa), (sb, fb), (ra, la), (rb, lb))):
        low[2 * BLOCK * n : 2 * BLOCK * (n + 1)] = one[0 : 2 * BLOCK]
        line[2 * BLOCK * n : 2 * BLOCK * (n + 1)] = two[0 : 2 * BLOCK]
    first = core[0] == 0
    s = [p[2 * BLOCK : FRONT].astype(F32) for p in (sa, ra, fa, la)]
    m = [earlier[0, p].astype(F32) for p in range(SIDE)]
    before = s[1] * m[1] + s[2] * m[2] + s[3] * m[3]
    total = s[0] + s[1] + s[2] + s[3]
    line[MID : MID + HALF] = jnp.where(first, total, s[0]).astype(BF)
    line[MID + HALF : MID + 2 * HALF] = jnp.where(first, 0.0, before).astype(BF)
    local[...] = before


def prefix_kernel(earlier, local, right, far, left, *rest):
    out, scratch, sems = rest[-3:]
    got = [
        pltpu.make_async_copy(piece.at[pl.ds(MID, 2 * HALF)], scratch.at[n], sems.at[n])
        for n, piece in enumerate((right, far, left))
    ]
    for copy in got:
        copy.start()
    for copy in got:
        copy.wait()
    total = local[...]
    for n in range(3):
        total = total + scratch[n, 0:HALF].astype(F32) * earlier[1, n + 1].astype(F32)
        total = total + scratch[n, HALF:].astype(F32)
    out[...] = total


def prefix(earlier, local, right, far, left, deps):
    return pl.pallas_call(
        prefix_kernel,
        in_specs=[SM, VM] + [ANY] * (3 + len(deps)),
        out_specs=VM,
        out_shape=jax.ShapeDtypeStruct((HALF, HD), F32),
        scratch_shapes=[pltpu.VMEM((3, 2 * HALF, HD), BF), pltpu.SemaphoreType.DMA((3,))],
        compiler_params=params(4),
        cost_estimate=cost(1e5, MIB // 2),
        name="prefix",
    )(earlier, local, right, far, left, *deps)


SPOTS = (0, BLOCK, FRONT, FRONT + BLOCK)


def placed(table, j, own_ref, peer_ref):
    a, b = table[0, j], table[1, j]
    first = own_ref[jnp.maximum(a, 0)].astype(F32) * jnp.where(a >= 0, 1.0, 0.0).astype(F32)
    second = peer_ref[jnp.maximum(b, 0)].astype(F32) * jnp.where(b >= 0, 1.0, 0.0).astype(F32)
    return first + second


def fill(table, own, peer, half, j, out, u, more=(), m=0):
    for q, spot in enumerate(SPOTS):
        at = pl.ds(spot, BLOCK)
        value = placed(table, 4 * j + q, own, peer)
        for ref in more:
            value = value + ref[m, at].astype(F32)
        out[u, at] = value.astype(BF)
    at = pl.ds(2 * BLOCK, HALF)
    value = half[...] * table[2, j].astype(F32)
    for ref in more:
        value = value + ref[m, at].astype(F32)
    out[u, at] = value.astype(BF)


def far_kernel(table, own, peer, half, far_a, far_b):
    @pl.loop(0, 2)
    def _(u):
        fill(table, own, peer, half, 8 + u, far_a, u)
        fill(table, own, peer, half, 10 + u, far_b, u)


def free_kernel(table, own, peer, half, right, left):
    @pl.loop(0, 2)
    def _(u):
        fill(table, own, peer, half, 6 + u, right, u)
        fill(table, own, peer, half, 12 + u, left, u)


def near_kernel(table, own, peer, half, ra, rb, right, left):
    @pl.loop(0, 2)
    def _(u):
        fill(table, own, peer, half, 4 + u, right, u, [ra], u)
        fill(table, own, peer, half, 14 + u, left, u, [rb], u)


def turn_kernel(table, own, peer, half, rl, rh, ll, lh, home, right_a, right_b, far_a, far_b, left_a, left_b, unit):
    @pl.loop(0, 2)
    def _(u):
        fill(table, own, peer, half, u, unit, u, [rl, ll], u)
        fill(table, own, peer, half, 2 + u, unit, 2 + u, [rh, lh], u)

    home[...] = unit[0]
    for n, (a, b) in ((1, (right_a, right_b)), (2, (far_a, far_b)), (3, (left_a, left_b))):
        a[...] = unit[n, 0:FRONT]
        b[...] = unit[n, FRONT:]


def last_kernel(right, left, ra, rb, o_right, o_left):
    o_right[...] = (right[...].astype(F32) + ra[...].astype(F32)).astype(BF)
    o_left[...] = (left[...].astype(F32) + rb[...].astype(F32)).astype(BF)


def tail_kernel(home, ra, rb, la, lb, mine, sent, extra):
    front = home[0:FRONT].astype(F32) + ra[...].astype(F32) + la[...].astype(F32)
    mine[...] = front[0 : 2 * BLOCK].astype(BF)
    extra[...] = front[2 * BLOCK :]
    sent[2 * BLOCK :] = front[2 * BLOCK :].astype(BF)
    back = home[FRONT:].astype(F32) + rb[...].astype(F32) + lb[...].astype(F32)
    sent[0 : 2 * BLOCK] = back.astype(BF)


def finish_kernel(core, k_ref, v_ref, dk, dv, mine_ref, got_ref, tail_ref, extra, adj, peer, kg, vg, scratch):
    first = core[0] == 0
    mine, got = mine_ref[...].astype(F32), got_ref[...].astype(F32)
    at = pl.ds(LIN * HD, HD)
    kg[:, at] = (dk[:, at] + jnp.where(first, mine, got)).astype(BF)
    vg[:, at] = (dv[:, at] + jnp.where(first, got, mine)).astype(BF)
    tail = tail_ref[...].astype(F32)
    scratch[0:HALF] = jnp.where(first, extra[...], tail)
    scratch[HALF:] = jnp.where(first, tail, extra[...])
    inner = jnp.where(pl.program_id(0) == 0, 1.0, 0.0).astype(F32)
    chip = jnp.where(first, 1.0, 0.0).astype(F32)
    for h in range(LIN):
        at = pl.ds(h * HD, HD)
        state = scratch[at, :] + peer[at, :].astype(F32) * chip + adj[1, h] * inner
        hi, lo = split(state)
        k, v = k_ref[:, at], v_ref[:, at]
        kg[:, at] = (dk[:, at] + dot(v, hi, 1, 1) + dot(v, lo, 1, 1)).astype(BF)
        vg[:, at] = (dv[:, at] + dot(k, hi, 1, 0) + dot(k, lo, 1, 0)).astype(BF)


def finish(core, keys, values, dk, dv, mine, got, extra, adjoints, peer):
    rows = pl.BlockSpec((BLOCK, keys.shape[1]), lambda i, c: (i, 0))
    piece = pl.BlockSpec((BLOCK, HD), lambda i, c: (i, 0))
    fixed = [
        pl.BlockSpec((HALF, HD), lambda i, c: (0, 0)),
        pl.BlockSpec(adjoints.shape, lambda i, c: (0, 0, 0, 0)),
        pl.BlockSpec((LIN * HD, HD), lambda i, c: (0, 0)),
    ]
    shape = jax.ShapeDtypeStruct(keys.shape, BF)
    return pl.pallas_call(
        finish_kernel,
        grid_spec=pltpu.PrefetchScalarGridSpec(
            num_scalar_prefetch=1,
            grid=(2,),
            in_specs=[rows] * 4 + [piece, piece, fixed[0]] + fixed,
            out_specs=[rows, rows],
            scratch_shapes=[pltpu.VMEM((LIN * HD, HD), F32)],
        ),
        out_shape=[shape, shape],
        compiler_params=params(32),
        cost_estimate=cost(5e8, 9 * MIB),
        name="finish",
    )(core, keys, values, dk, dv, mine, got, got[2 * BLOCK :], extra, adjoints, peer)


def where_is(blocks, place):
    owner, within = blocks // 2, blocks % 2
    pz = (place // (SIDE * CORES) - owner // (SIDE * CORES)) % SIDE
    px = (place // CORES % SIDE - owner // CORES % SIDE) % SIDE
    return pz, px, owner % CORES, within


def spot_of(blocks, place, stream):
    pz, px, core, within = where_is(blocks, place)
    rel = (core != stream).astype(jnp.int32)
    outer = jnp.where(stream == 0, pz, px)
    first = jnp.where(stream == 0, px, pz)
    return outer, first, rel * 2 + within


def spot_of(blocks, place, stream):
    pz, px, core, within = where_is(blocks, place)
    rel = (core != stream).astype(jnp.int32)
    outer = jnp.where(stream == 0, pz, px)
    first = jnp.where(stream == 0, px, pz)
    return outer, first, rel * 2 + within


def piece_of(blocks, place, stream):
    outer, first, rest = spot_of(blocks, place, stream)
    index = first % 2 * 16 + rest * 4
    return outer * 2 + first // 2 + 8 * (place % CORES != stream).astype(jnp.int32), index


def fetch_table(lists, place):
    flat = lists.reshape(-1)
    mine = place * 2 + jnp.arange(2 * LISTED, dtype=jnp.int32) // LISTED
    usable = (flat != mine).astype(jnp.int32)
    columns = [*piece_of(flat, place, 0), *piece_of(flat, place, 1), usable]
    return jnp.stack(columns, axis=1).astype(jnp.int32)


def back_table(lists, peer_lists, place):
    slots = jnp.arange(2 * LISTED, dtype=jnp.int32)[:, None]
    spots = jnp.arange(64, dtype=jnp.int32)[None, :]
    rows = []
    for some in (lists, peer_lists):
        outer, first, rest = spot_of(some.reshape(-1), place, place % CORES)
        target = (-outer) % SIDE * 16 + (-first) % SIDE * 4 + rest
        rows.append(jnp.max(jnp.where(target[:, None] == spots, slots, -1), axis=0))
    z, x = place // (SIDE * CORES), place // CORES % SIDE
    step = jnp.arange(64, dtype=jnp.int32)
    outer, inner = step // SIDE, step % SIDE
    on_keys = place % CORES == 0
    to_z = (z + jnp.where(on_keys, outer, inner)) % SIDE
    to_x = (x + jnp.where(on_keys, inner, outer)) % SIDE
    rows.append((to_z * SIDE + to_x < z * SIDE + x).astype(jnp.int32))
    return jnp.stack(rows).astype(jnp.int32)


def earlier_table(place):
    z, x = place // (SIDE * CORES), place // CORES % SIDE
    on_keys = place % CORES == 0
    first, second = jnp.where(on_keys, x, z), jnp.where(on_keys, z, x)
    step = jnp.arange(SIDE, dtype=jnp.int32)
    rows = [(c - step) % SIDE < c for c in (first, second)]
    return jnp.stack(rows).astype(jnp.int32)


def local(queries, keys, values, out_weight, out_grad, long_blocks):
    place = lax.axis_index("ctx").astype(jnp.int32)
    core = (place % CORES).reshape(1)
    row_count = queries.shape[0]
    positions = place * row_count + jnp.arange(row_count, dtype=jnp.int32)
    scale = 1.0 / (math.sqrt(HD) * jnp.sqrt((positions + 1).astype(F32)))
    scale = jnp.broadcast_to(scale[None, :], (8, row_count))
    lists = lax.dynamic_slice_in_dim(long_blocks, place * 2, 2, 0)
    peer_lists = lax.dynamic_slice_in_dim(long_blocks, (place ^ 1) * 2, 2, 0)
    fetch = fetch_table(lists, place)
    back = back_table(lists, peer_lists, place)
    earlier = earlier_table(place)

    grad_all = lax.all_gather(out_grad, "head", axis=1, tiled=True)

    states, mine, sent = whole_call(
        begin_kernel,
        [core],
        [keys, values],
        [((2, LIN, HD, HD), F32), ((2 * BLOCK, HD), BF), ((2 * BLOCK + LIN * HD, HD), BF)],
        "begin",
    )
    got = swap(sent)
    sa, sb = whole_call(
        start_kernel, [core], [mine, got, states], [((FRONT, HD), BF), ((2 * BLOCK, HD), BF)], "start",
        scratch=[pltpu.VMEM((LIN * HD, HD), F32)],
    )
    ra, lb = ring_move(sa, 0, 1), ring_move(sb, 0, -1)
    rb, la = ring_move(sb, 0, 1), ring_move(sa, 0, -1)
    fa, fb = ring_move(ra, 0, 1), ring_move(lb, 0, -1)
    low, high, inside = whole_call(
        line_kernel, [core, earlier], [sa, sb, ra, rb, fa, fb, la, lb],
        [((MID, HD), BF), ((MID + 2 * HALF, HD), BF), ((HALF, HD), F32)], "line",
    )
    low_right, low_left = ring_move(low, 1, 1), ring_move(low, 1, -1)
    high_left, high_right = ring_move(high, 1, -1), ring_move(high, 1, 1)
    low_far, high_far = ring_move(low_right, 1, 1), ring_move(high_left, 1, -1)
    pieces = [low, high, low_right, high_right, low_far, high_far, low_left, high_left]
    swapped = [swap(p) for p in pieces]
    pieces = pieces + swapped
    done = [low_far, low_left, *swapped[:4], *swapped[6:]]
    part = prefix(earlier, inside, high_right, high_far, high_left, done)
    other = swap(part)
    on_keys = place % CORES == 0
    chip = jnp.where(on_keys, jnp.concatenate([part, other]), jnp.concatenate([other, part]))
    chip = chip + jnp.where(on_keys, 0.0, got[2 * BLOCK :].astype(F32))
    chip = chip.reshape(LIN, HD, HD)
    before = jnp.stack([chip, chip + states[0]])

    sparse_out, probs, far_k, far_v, inverse = sparse_forward(fetch, queries, keys, values, pieces)
    attention = linear_forward(queries, keys, values, scale, before, sparse_out)
    partial_out = dot(attention, out_weight, 1, 1).astype(BF)
    layer_out = lax.psum_scatter(partial_out, "head", scatter_dimension=1, tiled=True)
    sparse_grad = dot(grad_all, out_weight[:, LIN * HD :], 1, 0).astype(BF)
    linear_grad = dot(grad_all, out_weight[:, : LIN * HD], 1, 0).astype(BF)
    query_grad, own_dk, own_dv, pair_mine, pair_sent = sparse_backward(
        core, queries, keys, values, sparse_grad, attention, probs, far_k, far_v, inverse
    )

    adjoints = block_adjoints(queries, linear_grad, scale)
    adjoint = (adjoints[0] + adjoints[1]).reshape(LIN * HD, HD)
    adjoint_peer = swap(adjoint.astype(BF))
    half = lax.dynamic_slice_in_dim(
        adjoint + adjoint_peer.astype(F32), place % CORES * HALF, HALF, 0
    )
    base = [pair_mine, swap(pair_sent), half]
    far_a, far_b = whole_call(
        far_kernel, [back], base, [((2, UNIT, HD), BF)] * 2, "back_far"
    )
    ra, rb = ring_move(far_a, 1, 1), ring_move(far_b, 1, -1)
    pair = [((2, UNIT, HD), BF)] * 2
    free = whole_call(free_kernel, [back], base, pair, "back_free", deps=[far_a])
    rh, ll = ring_move(free[0], 1, 1), ring_move(free[1], 1, -1)
    near = whole_call(near_kernel, [back], base + [ra, rb], pair, "back_near")
    rl, lh = ring_move(near[0], 1, 1), ring_move(near[1], 1, -1)
    query_grad, own_dk, own_dv = linear_backward(
        queries, keys, values, linear_grad, scale, before, (query_grad, own_dk, own_dv), inside
    )

    front, rear = ((FRONT, HD), BF), ((2 * BLOCK, HD), BF)
    home, right_a, right_b, far_a, far_b, left_a, left_b = whole_call(
        turn_kernel, [back], base + [rl, rh, ll, lh], [((UNIT, HD), BF)] + [front, rear] * 3,
        "back_turn", deps=[query_grad], scratch=[pltpu.VMEM((SIDE, UNIT, HD), BF)],
    )
    ra, rb = ring_move(far_a, 0, 1), ring_move(far_b, 0, -1)
    to_rb, to_la = ring_move(right_b, 0, 1), ring_move(left_a, 0, -1)
    right_a, left_b = whole_call(last_kernel, [], [right_a, left_b, ra, rb], [front, rear], "back_last")
    to_ra, to_lb = ring_move(right_a, 0, 1), ring_move(left_b, 0, -1)
    mine, sent, extra = whole_call(
        tail_kernel, [], [home, to_ra, to_rb, to_la, to_lb],
        [rear, front, ((HALF, HD), F32)], "back_tail",
    )
    key_grad, value_grad = finish(
        core, keys, values, own_dk, own_dv, mine, swap(sent), extra, adjoints, adjoint_peer
    )
    return layer_out, query_grad, key_grad, value_grad


def solution(mesh):
    return jax.shard_map(
        local,
        mesh=mesh,
        in_specs=(
            P("ctx", "head"),
            P("ctx", "head"),
            P("ctx", "head"),
            P(None, "head"),
            P("ctx", "head"),
            P(),
        ),
        out_specs=(P("ctx", "head"), P("ctx", "head"), P("ctx", "head"), P("ctx", "head")),
        check_vma=False,
    )
```

```python
import functools
import math

import jax
import jax.numpy as jnp
from jax import lax
from jax.experimental import pallas as pl
from jax.experimental.pallas import tpu as pltpu
from jax.sharding import PartitionSpec as P

HD = 128
LIN = 3
LISTED = 4
BLOCK = 512
SIDE = 4
CORES = 2
CTX = SIDE * SIDE * CORES
SCALING = 1.0 / math.sqrt(HD)
BF = jnp.bfloat16
F32 = jnp.float32
MIB = 1 << 20
COSTS = 1.0
HALF = LIN * HD // CORES
UNIT = 4 * BLOCK + HALF
FRONT = 2 * BLOCK + HALF
MID = 8 * BLOCK
TILE = (BLOCK, HD)


def dot(a, b, ca, cb):
    return lax.dot_general(a, b, (((ca,), (cb,)), ((), ())), preferred_element_type=F32)


def params(mib):
    return pltpu.CompilerParams(vmem_limit_bytes=mib * MIB)


def cost(flops, nbytes):
    return pl.CostEstimate(flops=int(flops * COSTS), bytes_accessed=int(nbytes * COSTS), transcendentals=0)


def ring_move(value, axis, step):
    pairs = []
    for z in range(SIDE):
        for x in range(SIDE):
            for c in range(CORES):
                dx, dz = (step, 0) if axis == c else (0, step)
                to = (((z + dz) % SIDE) * SIDE + (x + dx) % SIDE) * CORES + c
                pairs.append(((z * SIDE + x) * CORES + c, to))
    return lax.ppermute(value, "ctx", pairs)


def swap(value):
    return lax.ppermute(value, "ctx", [(i, i ^ 1) for i in range(CTX)])


def drop(kernel, n_in, n_deps, *refs):
    kernel(*refs[:n_in], *refs[n_in + n_deps :])


ANY = pl.BlockSpec(memory_space=pl.ANY)
VM = pl.BlockSpec(memory_space=pltpu.VMEM)
SM = pl.BlockSpec(memory_space=pltpu.SMEM)


def whole_call(kernel, scalars, operands, outs, name, deps=(), scratch=(), flops=1e6):
    outs = [jax.ShapeDtypeStruct(*o) for o in outs]
    nbytes = sum(math.prod(o.shape) * o.dtype.itemsize for o in [*operands, *outs])
    n_in = len(scalars) + len(operands)
    return pl.pallas_call(
        functools.partial(drop, kernel, n_in, len(deps)),
        in_specs=[SM] * len(scalars) + [VM] * len(operands) + [ANY] * len(deps),
        out_specs=[VM] * len(outs),
        out_shape=outs,
        scratch_shapes=list(scratch),
        compiler_params=params(32),
        cost_estimate=cost(flops, nbytes),
        name=name,
    )(*scalars, *operands, *deps)


def causal_mask():
    s = lax.broadcasted_iota(jnp.int32, (BLOCK, BLOCK), 0)
    u = lax.broadcasted_iota(jnp.int32, (BLOCK, BLOCK), 1)
    return s <= u


def adjoint_kernel(q_ref, g_ref, c_ref, out_ref):
    qt = (q_ref[...].astype(F32).T * c_ref[0:1, :]).astype(BF)
    out_ref[0, 0] = dot(qt, g_ref[...], 1, 0)


def tile_spec():
    return pl.BlockSpec(TILE, lambda i, h: (i, h))


def scale_spec():
    return pl.BlockSpec((8, BLOCK), lambda i, h: (0, i))


def state_spec():
    return pl.BlockSpec((1, 1, HD, HD), lambda i, h: (i, h, 0, 0))


def block_adjoints(queries, grads, scale):
    return pl.pallas_call(
        adjoint_kernel,
        grid=(2, LIN),
        in_specs=[tile_spec(), tile_spec(), scale_spec()],
        out_specs=state_spec(),
        out_shape=jax.ShapeDtypeStruct((2, LIN, HD, HD), F32),
        compiler_params=params(16),
        cost_estimate=cost(1e8, 2 * MIB),
        name="block_adjoints",
    )(queries, grads, scale)


def split(value):
    high = value.astype(BF)
    return high, (value - high.astype(F32)).astype(BF)


def linear_forward_kernel(q_ref, k_ref, v_ref, c_ref, s_ref, base_ref, out_ref):
    q, k, v, c = q_ref[...], k_ref[...], v_ref[...], c_ref[0:1, :]
    weights = jnp.where(causal_mask(), dot(k, q, 1, 1) * c, 0.0).astype(BF)
    hi, lo = split(s_ref[0, 0].T)
    out = dot(v, weights, 0, 0) + c * (dot(hi, q, 1, 1) + dot(lo, q, 1, 1))
    out_ref[...] = out.T.astype(BF)


def linear_forward(queries, keys, values, scale, before, base):
    return pl.pallas_call(
        linear_forward_kernel,
        grid=(2, LIN),
        in_specs=[tile_spec()] * 3 + [scale_spec(), state_spec(), ANY],
        out_specs=tile_spec(),
        out_shape=jax.ShapeDtypeStruct(queries.shape, BF),
        input_output_aliases={5: 0},
        compiler_params=params(12),
        cost_estimate=cost(2.4e9, 4 * MIB),
        name="linear_forward",
    )(queries, keys, values, scale, before, base)


def linear_backward_kernel(
    q_ref, k_ref, v_ref, g_ref, c_ref, s_ref, b0, b1, b2, dep, dq_ref, dk_ref, dv_ref
):
    q, k, v, g, c = q_ref[...], k_ref[...], v_ref[...], g_ref[...], c_ref[0:1, :]
    mask = causal_mask()
    grad_weights = jnp.where(mask, dot(v, g, 1, 1) * c, 0.0).astype(BF)
    hi, lo = split(s_ref[0, 0])
    dq = dot(k, grad_weights, 0, 0) + c * (dot(hi, g, 1, 1) + dot(lo, g, 1, 1))
    dq_ref[...] = dq.T.astype(BF)
    dk_ref[...] = dot(grad_weights, q, 1, 0)
    weights = jnp.where(mask, dot(k, q, 1, 1) * c, 0.0).astype(BF)
    dv_ref[...] = dot(weights, g, 1, 0)


def linear_backward(queries, keys, values, grads, scale, before, bases, dep):
    shape = queries.shape
    return pl.pallas_call(
        linear_backward_kernel,
        grid=(2, LIN),
        in_specs=[tile_spec()] * 4 + [scale_spec(), state_spec()] + [ANY] * 4,
        out_specs=[tile_spec()] * 3,
        out_shape=[jax.ShapeDtypeStruct(shape, t) for t in (BF, F32, F32)],
        input_output_aliases={6: 0, 7: 1, 8: 2},
        compiler_params=params(16),
        cost_estimate=cost(5e9, 9 * MIB),
        name="linear_backward",
    )(queries, keys, values, grads, scale, before, *bases, dep)


PIECES = 16


def sparse_forward_kernel(table, q_ref, k_ref, v_ref, *rest):
    pieces = rest[:PIECES]
    out_ref, kf_ref, vf_ref, log_ref, s_ref, sems = rest[PIECES:]
    step = pl.program_id(0)

    @pl.when(step == 0)
    def _():
        @pl.loop(0, 2 * LISTED)
        def _(row):
            for j in range(PIECES):
                for n, far in ((0, kf_ref), (1, vf_ref)):

                    @pl.when(table[row, 2 * n] == j)
                    def _():
                        at = pl.ds(pl.multiple_of(table[row, 2 * n + 1] * HD, HD), BLOCK)
                        pltpu.make_async_copy(pieces[j].at[at], far.at[row], sems.at[n, row]).start()

    q = q_ref[...]
    s = jnp.where(causal_mask(), dot(k_ref[...], q, 1, 1) * SCALING, -1e30)
    s_ref[0] = s
    peak = jnp.max(s, axis=0, keepdims=True)
    for r in range(LISTED):
        row = step * LISTED + r
        pltpu.make_async_copy(pieces[0].at[pl.ds(0, BLOCK)], kf_ref.at[row], sems.at[0, row]).wait()
        bias = jnp.where(table[row, 4] == 1, 0.0, -1e30).astype(F32)
        s = dot(kf_ref[row], q, 1, 1) * SCALING + bias
        s_ref[r + 1] = s
        peak = jnp.maximum(peak, jnp.max(s, axis=0, keepdims=True))
    total = jnp.zeros((1, BLOCK), F32)
    out = jnp.zeros((HD, BLOCK), F32)
    for r in range(LISTED + 1):
        e = jnp.exp(s_ref[r] - peak)
        total = total + jnp.sum(e, axis=0, keepdims=True)
        p = e.astype(BF)
        if r == 0:
            value = v_ref[...]
        else:
            row = step * LISTED + r - 1
            pltpu.make_async_copy(pieces[0].at[pl.ds(0, BLOCK)], vf_ref.at[row], sems.at[1, row]).wait()
            value = vf_ref[row]
        out = out + dot(value, p, 0, 0)
    log_ref[...] = jnp.broadcast_to(peak + jnp.log(total), (8, BLOCK))
    out_ref[...] = (out / total).T.astype(BF)


def sparse_forward(table, queries, keys, values, pieces):
    column = pl.BlockSpec(TILE, lambda i, t: (i, LIN))
    far = (2 * LISTED, BLOCK, HD)
    return pl.pallas_call(
        sparse_forward_kernel,
        grid_spec=pltpu.PrefetchScalarGridSpec(
            num_scalar_prefetch=1,
            grid=(2,),
            in_specs=[column] * 3 + [ANY] * PIECES,
            out_specs=[
                column,
                pl.BlockSpec(far, lambda i, t: (0, 0, 0)),
                pl.BlockSpec(far, lambda i, t: (0, 0, 0)),
                pl.BlockSpec((8, BLOCK), lambda i, t: (0, i)),
            ],
            scratch_shapes=[
                pltpu.VMEM((LISTED + 1, BLOCK, BLOCK), F32),
                pltpu.SemaphoreType.DMA((2, 2 * LISTED)),
            ],
        ),
        out_shape=[
            jax.ShapeDtypeStruct(queries.shape, BF),
            jax.ShapeDtypeStruct(far, BF),
            jax.ShapeDtypeStruct(far, BF),
            jax.ShapeDtypeStruct((8, queries.shape[0]), F32),
        ],
        compiler_params=params(20),
        cost_estimate=cost(4e9, 12 * MIB),
        name="sparse_forward",
    )(table, queries, keys, values, *pieces)


def sparse_backward_kernel(
    core, table, q_ref, k_ref, v_ref, g_ref, o_ref, kf_ref, vf_ref, log_ref, dq_ref, dk_ref, dv_ref, mine_ref, sent_ref
):
    first = core[0] == 0
    q, g = q_ref[...], g_ref[...]
    row_dot = jnp.sum((g.astype(F32) * o_ref[...].astype(F32)).T, axis=0, keepdims=True)
    logs = log_ref[0:1, :]
    dq = jnp.zeros((HD, BLOCK), F32)
    for r in range(LISTED + 1):
        key = k_ref[...] if r == 0 else kf_ref[r - 1]
        value = v_ref[...] if r == 0 else vf_ref[r - 1]
        s = dot(key, q, 1, 1) * SCALING
        if r == 0:
            p = jnp.exp(jnp.where(causal_mask(), s - logs, -1e30))
        else:
            used = table[pl.program_id(0) * LISTED + r - 1, 4] == 1
            p = jnp.exp(s - jnp.where(used, logs, 1e30))
        ds = (p * (dot(value, g, 1, 1) - row_dot)).astype(BF)
        dq = dq + dot(key, ds, 0, 0)
        dk = dot(ds, q, 1, 0) * SCALING
        dv = dot(p.astype(BF), g, 1, 0)
        if r == 0:
            dk_ref[...] = dk
            dv_ref[...] = dv
        else:
            mine_ref[r - 1] = jnp.where(first, dk, dv).astype(BF)
            sent_ref[r - 1] = jnp.where(first, dv, dk).astype(BF)
    dq_ref[...] = (dq * SCALING).T.astype(BF)


def sparse_backward(core, table, queries, keys, values, grads, outs, far_k, far_v, logs):
    column = pl.BlockSpec(TILE, lambda i, c, t: (i, LIN))
    four = pl.BlockSpec((LISTED, BLOCK, HD), lambda i, c, t: (i, 0, 0))
    return pl.pallas_call(
        sparse_backward_kernel,
        grid_spec=pltpu.PrefetchScalarGridSpec(
            num_scalar_prefetch=2,
            grid=(2,),
            in_specs=[column] * 3
            + [pl.BlockSpec(TILE, lambda i, c, t: (i, 0)), column, four, four]
            + [pl.BlockSpec((8, BLOCK), lambda i, c, t: (0, i))],
            out_specs=[column, column, column, four, four],
        ),
        out_shape=[
            jax.ShapeDtypeStruct(queries.shape, BF),
            jax.ShapeDtypeStruct(queries.shape, F32),
            jax.ShapeDtypeStruct(queries.shape, F32),
            jax.ShapeDtypeStruct((2 * LISTED, BLOCK, HD), BF),
            jax.ShapeDtypeStruct((2 * LISTED, BLOCK, HD), BF),
        ],
        compiler_params=params(20),
        cost_estimate=cost(8e9, 8 * MIB),
        name="sparse_backward",
    )(core, table, queries, keys, values, grads, outs, far_k, far_v, logs)


def begin_kernel(core, k_ref, v_ref, states, mine, sent):
    first = core[0] == 0
    for h in range(LIN):
        at = pl.ds(h * HD, HD)
        s0 = dot(k_ref[0:BLOCK, at], v_ref[0:BLOCK, at], 0, 0)
        s1 = dot(k_ref[BLOCK:, at], v_ref[BLOCK:, at], 0, 0)
        states[0, h] = s0
        states[1, h] = s1
        sent[2 * BLOCK + h * HD : 2 * BLOCK + (h + 1) * HD] = (s0 + s1).astype(BF)
    at = pl.ds(LIN * HD, HD)
    k, v = k_ref[:, at], v_ref[:, at]
    mine[...] = jnp.where(first, k, v)
    sent[0 : 2 * BLOCK] = jnp.where(first, v, k)


def start_kernel(core, mine, got, states, out, rest, scratch):
    out[0 : 2 * BLOCK] = mine[...]
    rest[...] = got[0 : 2 * BLOCK]
    for h in range(LIN):
        other = got[2 * BLOCK + h * HD : 2 * BLOCK + (h + 1) * HD].astype(F32)
        scratch[h * HD : (h + 1) * HD] = states[0, h] + states[1, h] + other
    out[2 * BLOCK : FRONT] = scratch[pl.ds(pl.multiple_of(core[0] * HALF, HALF), HALF)].astype(BF)


def line_kernel(core, earlier, sa, sb, ra, rb, fa, fb, la, lb, low, line, local):
    for n, (one, two) in enumerate(((sa, fa), (sb, fb), (ra, la), (rb, lb))):
        low[2 * BLOCK * n : 2 * BLOCK * (n + 1)] = one[0 : 2 * BLOCK]
        line[2 * BLOCK * n : 2 * BLOCK * (n + 1)] = two[0 : 2 * BLOCK]
    first = core[0] == 0
    s = [p[2 * BLOCK : FRONT].astype(F32) for p in (sa, ra, fa, la)]
    m = [earlier[0, p].astype(F32) for p in range(SIDE)]
    before = s[1] * m[1] + s[2] * m[2] + s[3] * m[3]
    total = s[0] + s[1] + s[2] + s[3]
    line[MID : MID + HALF] = jnp.where(first, total, s[0]).astype(BF)
    line[MID + HALF : MID + 2 * HALF] = jnp.where(first, 0.0, before).astype(BF)
    local[...] = before


def prefix_kernel(earlier, local, right, far, left, *rest):
    out, scratch, sems = rest[-3:]
    got = [
        pltpu.make_async_copy(piece.at[pl.ds(MID, 2 * HALF)], scratch.at[n], sems.at[n])
        for n, piece in enumerate((right, far, left))
    ]
    for copy in got:
        copy.start()
    for copy in got:
        copy.wait()
    total = local[...]
    for n in range(3):
        total = total + scratch[n, 0:HALF].astype(F32) * earlier[1, n + 1].astype(F32)
        total = total + scratch[n, HALF:].astype(F32)
    out[...] = total


def prefix(earlier, local, right, far, left, deps):
    return pl.pallas_call(
        prefix_kernel,
        in_specs=[SM, VM] + [ANY] * (3 + len(deps)),
        out_specs=VM,
        out_shape=jax.ShapeDtypeStruct((HALF, HD), F32),
        scratch_shapes=[pltpu.VMEM((3, 2 * HALF, HD), BF), pltpu.SemaphoreType.DMA((3,))],
        compiler_params=params(4),
        cost_estimate=cost(1e5, MIB // 2),
        name="prefix",
    )(earlier, local, right, far, left, *deps)


SPOTS = (0, BLOCK, FRONT, FRONT + BLOCK)


def placed(table, j, own_ref, peer_ref):
    a, b = table[0, j], table[1, j]
    first = own_ref[jnp.maximum(a, 0)].astype(F32) * jnp.where(a >= 0, 1.0, 0.0).astype(F32)
    second = peer_ref[jnp.maximum(b, 0)].astype(F32) * jnp.where(b >= 0, 1.0, 0.0).astype(F32)
    return first + second


def fill(table, own, peer, half, j, out, u, more=(), m=0):
    for q, spot in enumerate(SPOTS):
        at = pl.ds(spot, BLOCK)
        value = placed(table, 4 * j + q, own, peer)
        for ref in more:
            value = value + ref[m, at].astype(F32)
        out[u, at] = value.astype(BF)
    at = pl.ds(2 * BLOCK, HALF)
    value = half[...] * table[2, j].astype(F32)
    for ref in more:
        value = value + ref[m, at].astype(F32)
    out[u, at] = value.astype(BF)


def far_kernel(table, own, peer, half, far_a, far_b):
    @pl.loop(0, 2)
    def _(u):
        fill(table, own, peer, half, 8 + u, far_a, u)
        fill(table, own, peer, half, 10 + u, far_b, u)


def free_kernel(table, own, peer, half, right, left):
    @pl.loop(0, 2)
    def _(u):
        fill(table, own, peer, half, 6 + u, right, u)
        fill(table, own, peer, half, 12 + u, left, u)


def near_kernel(table, own, peer, half, ra, rb, right, left):
    @pl.loop(0, 2)
    def _(u):
        fill(table, own, peer, half, 4 + u, right, u, [ra], u)
        fill(table, own, peer, half, 14 + u, left, u, [rb], u)


def turn_kernel(table, own, peer, half, rl, rh, ll, lh, home, right_a, right_b, far_a, far_b, left_a, left_b, unit):
    @pl.loop(0, 2)
    def _(u):
        fill(table, own, peer, half, u, unit, u, [rl, ll], u)
        fill(table, own, peer, half, 2 + u, unit, 2 + u, [rh, lh], u)

    home[...] = unit[0]
    for n, (a, b) in ((1, (right_a, right_b)), (2, (far_a, far_b)), (3, (left_a, left_b))):
        a[...] = unit[n, 0:FRONT]
        b[...] = unit[n, FRONT:]


def last_kernel(right, left, ra, rb, o_right, o_left):
    o_right[...] = (right[...].astype(F32) + ra[...].astype(F32)).astype(BF)
    o_left[...] = (left[...].astype(F32) + rb[...].astype(F32)).astype(BF)


def tail_kernel(home, ra, rb, la, lb, mine, sent, extra):
    front = home[0:FRONT].astype(F32) + ra[...].astype(F32) + la[...].astype(F32)
    mine[...] = front[0 : 2 * BLOCK].astype(BF)
    extra[...] = front[2 * BLOCK :]
    sent[2 * BLOCK :] = front[2 * BLOCK :].astype(BF)
    back = home[FRONT:].astype(F32) + rb[...].astype(F32) + lb[...].astype(F32)
    sent[0 : 2 * BLOCK] = back.astype(BF)


def finish_kernel(core, k_ref, v_ref, dk, dv, mine_ref, got_ref, tail_ref, extra, adj, peer, kg, vg, scratch):
    first = core[0] == 0
    mine, got = mine_ref[...].astype(F32), got_ref[...].astype(F32)
    at = pl.ds(LIN * HD, HD)
    kg[:, at] = (dk[:, at] + jnp.where(first, mine, got)).astype(BF)
    vg[:, at] = (dv[:, at] + jnp.where(first, got, mine)).astype(BF)
    tail = tail_ref[...].astype(F32)
    scratch[0:HALF] = jnp.where(first, extra[...], tail)
    scratch[HALF:] = jnp.where(first, tail, extra[...])
    inner = jnp.where(pl.program_id(0) == 0, 1.0, 0.0).astype(F32)
    chip = jnp.where(first, 1.0, 0.0).astype(F32)
    for h in range(LIN):
        at = pl.ds(h * HD, HD)
        state = scratch[at, :] + peer[at, :].astype(F32) * chip + adj[1, h] * inner
        hi, lo = split(state)
        k, v = k_ref[:, at], v_ref[:, at]
        kg[:, at] = (dk[:, at] + dot(v, hi, 1, 1) + dot(v, lo, 1, 1)).astype(BF)
        vg[:, at] = (dv[:, at] + dot(k, hi, 1, 0) + dot(k, lo, 1, 0)).astype(BF)


def finish(core, keys, values, dk, dv, mine, got, extra, adjoints, peer):
    rows = pl.BlockSpec((BLOCK, keys.shape[1]), lambda i, c: (i, 0))
    piece = pl.BlockSpec((BLOCK, HD), lambda i, c: (i, 0))
    fixed = [
        pl.BlockSpec((HALF, HD), lambda i, c: (0, 0)),
        pl.BlockSpec(adjoints.shape, lambda i, c: (0, 0, 0, 0)),
        pl.BlockSpec((LIN * HD, HD), lambda i, c: (0, 0)),
    ]
    shape = jax.ShapeDtypeStruct(keys.shape, BF)
    return pl.pallas_call(
        finish_kernel,
        grid_spec=pltpu.PrefetchScalarGridSpec(
            num_scalar_prefetch=1,
            grid=(2,),
            in_specs=[rows] * 4 + [piece, piece, fixed[0]] + fixed,
            out_specs=[rows, rows],
            scratch_shapes=[pltpu.VMEM((LIN * HD, HD), F32)],
        ),
        out_shape=[shape, shape],
        compiler_params=params(32),
        cost_estimate=cost(5e8, 9 * MIB),
        name="finish",
    )(core, keys, values, dk, dv, mine, got, got[2 * BLOCK :], extra, adjoints, peer)


def where_is(blocks, place):
    owner, within = blocks // 2, blocks % 2
    pz = (place // (SIDE * CORES) - owner // (SIDE * CORES)) % SIDE
    px = (place // CORES % SIDE - owner // CORES % SIDE) % SIDE
    return pz, px, owner % CORES, within


def spot_of(blocks, place, stream):
    pz, px, core, within = where_is(blocks, place)
    rel = (core != stream).astype(jnp.int32)
    outer = jnp.where(stream == 0, pz, px)
    first = jnp.where(stream == 0, px, pz)
    return outer, first, rel * 2 + within


def spot_of(blocks, place, stream):
    pz, px, core, within = where_is(blocks, place)
    rel = (core != stream).astype(jnp.int32)
    outer = jnp.where(stream == 0, pz, px)
    first = jnp.where(stream == 0, px, pz)
    return outer, first, rel * 2 + within


def piece_of(blocks, place, stream):
    outer, first, rest = spot_of(blocks, place, stream)
    index = first % 2 * 16 + rest * 4
    return outer * 2 + first // 2 + 8 * (place % CORES != stream).astype(jnp.int32), index


def fetch_table(lists, place):
    flat = lists.reshape(-1)
    mine = place * 2 + jnp.arange(2 * LISTED, dtype=jnp.int32) // LISTED
    usable = (flat != mine).astype(jnp.int32)
    columns = [*piece_of(flat, place, 0), *piece_of(flat, place, 1), usable]
    return jnp.stack(columns, axis=1).astype(jnp.int32)


def back_table(lists, peer_lists, place):
    slots = jnp.arange(2 * LISTED, dtype=jnp.int32)[:, None]
    spots = jnp.arange(64, dtype=jnp.int32)[None, :]
    rows = []
    for some in (lists, peer_lists):
        outer, first, rest = spot_of(some.reshape(-1), place, place % CORES)
        target = (-outer) % SIDE * 16 + (-first) % SIDE * 4 + rest
        rows.append(jnp.max(jnp.where(target[:, None] == spots, slots, -1), axis=0))
    z, x = place // (SIDE * CORES), place // CORES % SIDE
    step = jnp.arange(64, dtype=jnp.int32)
    outer, inner = step // SIDE, step % SIDE
    on_keys = place % CORES == 0
    to_z = (z + jnp.where(on_keys, outer, inner)) % SIDE
    to_x = (x + jnp.where(on_keys, inner, outer)) % SIDE
    rows.append((to_z * SIDE + to_x < z * SIDE + x).astype(jnp.int32))
    return jnp.stack(rows).astype(jnp.int32)


def earlier_table(place):
    z, x = place // (SIDE * CORES), place // CORES % SIDE
    on_keys = place % CORES == 0
    first, second = jnp.where(on_keys, x, z), jnp.where(on_keys, z, x)
    step = jnp.arange(SIDE, dtype=jnp.int32)
    rows = [(c - step) % SIDE < c for c in (first, second)]
    return jnp.stack(rows).astype(jnp.int32)


def local(queries, keys, values, out_weight, out_grad, long_blocks):
    place = lax.axis_index("ctx").astype(jnp.int32)
    core = (place % CORES).reshape(1)
    row_count = queries.shape[0]
    positions = place * row_count + jnp.arange(row_count, dtype=jnp.int32)
    scale = 1.0 / (math.sqrt(HD) * jnp.sqrt((positions + 1).astype(F32)))
    scale = jnp.broadcast_to(scale[None, :], (8, row_count))
    lists = lax.dynamic_slice_in_dim(long_blocks, place * 2, 2, 0)
    peer_lists = lax.dynamic_slice_in_dim(long_blocks, (place ^ 1) * 2, 2, 0)
    fetch = fetch_table(lists, place)
    back = back_table(lists, peer_lists, place)
    earlier = earlier_table(place)

    grad_all = lax.all_gather(out_grad, "head", axis=1, tiled=True)

    states, mine, sent = whole_call(
        begin_kernel,
        [core],
        [keys, values],
        [((2, LIN, HD, HD), F32), ((2 * BLOCK, HD), BF), ((2 * BLOCK + LIN * HD, HD), BF)],
        "begin",
    )
    got = swap(sent)
    sa, sb = whole_call(
        start_kernel, [core], [mine, got, states], [((FRONT, HD), BF), ((2 * BLOCK, HD), BF)], "start",
        scratch=[pltpu.VMEM((LIN * HD, HD), F32)],
    )
    ra, lb = ring_move(sa, 0, 1), ring_move(sb, 0, -1)
    rb, la = ring_move(sb, 0, 1), ring_move(sa, 0, -1)
    fa, fb = ring_move(ra, 0, 1), ring_move(lb, 0, -1)
    low, high, inside = whole_call(
        line_kernel, [core, earlier], [sa, sb, ra, rb, fa, fb, la, lb],
        [((MID, HD), BF), ((MID + 2 * HALF, HD), BF), ((HALF, HD), F32)], "line",
    )
    low_right, low_left = ring_move(low, 1, 1), ring_move(low, 1, -1)
    high_left, high_right = ring_move(high, 1, -1), ring_move(high, 1, 1)
    low_far, high_far = ring_move(low_right, 1, 1), ring_move(high_left, 1, -1)
    pieces = [low, high, low_right, high_right, low_far, high_far, low_left, high_left]
    swapped = [swap(p) for p in pieces]
    pieces = pieces + swapped
    done = [low_far, low_left, *swapped[:4], *swapped[6:]]
    part = prefix(earlier, inside, high_right, high_far, high_left, done)
    other = swap(part)
    on_keys = place % CORES == 0
    chip = jnp.where(on_keys, jnp.concatenate([part, other]), jnp.concatenate([other, part]))
    chip = chip + jnp.where(on_keys, 0.0, got[2 * BLOCK :].astype(F32))
    chip = chip.reshape(LIN, HD, HD)
    before = jnp.stack([chip, chip + states[0]])

    sparse_out, far_k, far_v, logs = sparse_forward(fetch, queries, keys, values, pieces)
    attention = linear_forward(queries, keys, values, scale, before, sparse_out)
    partial_out = dot(attention, out_weight, 1, 1).astype(BF)
    layer_out = lax.psum_scatter(partial_out, "head", scatter_dimension=1, tiled=True)
    sparse_grad = dot(grad_all, out_weight[:, LIN * HD :], 1, 0).astype(BF)
    linear_grad = dot(grad_all, out_weight[:, : LIN * HD], 1, 0).astype(BF)
    query_grad, own_dk, own_dv, pair_mine, pair_sent = sparse_backward(
        core, fetch, queries, keys, values, sparse_grad, attention, far_k, far_v, logs
    )

    adjoints = block_adjoints(queries, linear_grad, scale)
    adjoint = (adjoints[0] + adjoints[1]).reshape(LIN * HD, HD)
    adjoint_peer = swap(adjoint.astype(BF))
    half = lax.dynamic_slice_in_dim(
        adjoint + adjoint_peer.astype(F32), place % CORES * HALF, HALF, 0
    )
    base = [pair_mine, swap(pair_sent), half]
    far_a, far_b = whole_call(
        far_kernel, [back], base, [((2, UNIT, HD), BF)] * 2, "back_far"
    )
    ra, rb = ring_move(far_a, 1, 1), ring_move(far_b, 1, -1)
    pair = [((2, UNIT, HD), BF)] * 2
    free = whole_call(free_kernel, [back], base, pair, "back_free", deps=[far_a])
    rh, ll = ring_move(free[0], 1, 1), ring_move(free[1], 1, -1)
    near = whole_call(near_kernel, [back], base + [ra, rb], pair, "back_near")
    rl, lh = ring_move(near[0], 1, 1), ring_move(near[1], 1, -1)
    query_grad, own_dk, own_dv = linear_backward(
        queries, keys, values, linear_grad, scale, before, (query_grad, own_dk, own_dv), inside
    )

    front, rear = ((FRONT, HD), BF), ((2 * BLOCK, HD), BF)
    home, right_a, right_b, far_a, far_b, left_a, left_b = whole_call(
        turn_kernel, [back], base + [rl, rh, ll, lh], [((UNIT, HD), BF)] + [front, rear] * 3,
        "back_turn", deps=[query_grad], scratch=[pltpu.VMEM((SIDE, UNIT, HD), BF)],
    )
    ra, rb = ring_move(far_a, 0, 1), ring_move(far_b, 0, -1)
    to_rb, to_la = ring_move(right_b, 0, 1), ring_move(left_a, 0, -1)
    right_a, left_b = whole_call(last_kernel, [], [right_a, left_b, ra, rb], [front, rear], "back_last")
    to_ra, to_lb = ring_move(right_a, 0, 1), ring_move(left_b, 0, -1)
    mine, sent, extra = whole_call(
        tail_kernel, [], [home, to_ra, to_rb, to_la, to_lb],
        [rear, front, ((HALF, HD), F32)], "back_tail",
    )
    key_grad, value_grad = finish(
        core, keys, values, own_dk, own_dv, mine, swap(sent), extra, adjoints, adjoint_peer
    )
    return layer_out, query_grad, key_grad, value_grad


def solution(mesh):
    return jax.shard_map(
        local,
        mesh=mesh,
        in_specs=(
            P("ctx", "head"),
            P("ctx", "head"),
            P("ctx", "head"),
            P(None, "head"),
            P("ctx", "head"),
            P(),
        ),
        out_specs=(P("ctx", "head"), P("ctx", "head"), P("ctx", "head"), P("ctx", "head")),
        check_vma=False,
    )
```

```python
import functools
import math

import jax
import jax.numpy as jnp
from jax import lax
from jax.experimental import pallas as pl
from jax.experimental.pallas import tpu as pltpu
from jax.sharding import PartitionSpec as P

HD = 128
LIN = 3
LISTED = 4
BLOCK = 512
SIDE = 4
CORES = 2
CTX = SIDE * SIDE * CORES
SCALING = 1.0 / math.sqrt(HD)
BF = jnp.bfloat16
F32 = jnp.float32
MIB = 1 << 20
COSTS = 1.0
HALF = LIN * HD // CORES
UNIT = 4 * BLOCK + HALF
FRONT = 2 * BLOCK + HALF
MID = 8 * BLOCK
TILE = (BLOCK, HD)


def dot(a, b, ca, cb):
    return lax.dot_general(a, b, (((ca,), (cb,)), ((), ())), preferred_element_type=F32)


def params(mib):
    return pltpu.CompilerParams(vmem_limit_bytes=mib * MIB)


def cost(flops, nbytes):
    return pl.CostEstimate(flops=int(flops * COSTS), bytes_accessed=int(nbytes * COSTS), transcendentals=0)


def ring_move(value, axis, step):
    pairs = []
    for z in range(SIDE):
        for x in range(SIDE):
            for c in range(CORES):
                dx, dz = (step, 0) if axis == c else (0, step)
                to = (((z + dz) % SIDE) * SIDE + (x + dx) % SIDE) * CORES + c
                pairs.append(((z * SIDE + x) * CORES + c, to))
    return lax.ppermute(value, "ctx", pairs)


def swap(value):
    return lax.ppermute(value, "ctx", [(i, i ^ 1) for i in range(CTX)])


def drop(kernel, n_in, n_deps, *refs):
    kernel(*refs[:n_in], *refs[n_in + n_deps :])


ANY = pl.BlockSpec(memory_space=pl.ANY)
VM = pl.BlockSpec(memory_space=pltpu.VMEM)
SM = pl.BlockSpec(memory_space=pltpu.SMEM)


def whole_call(kernel, scalars, operands, outs, name, deps=(), scratch=(), flops=1e6):
    outs = [jax.ShapeDtypeStruct(*o) for o in outs]
    nbytes = sum(math.prod(o.shape) * o.dtype.itemsize for o in [*operands, *outs])
    n_in = len(scalars) + len(operands)
    return pl.pallas_call(
        functools.partial(drop, kernel, n_in, len(deps)),
        in_specs=[SM] * len(scalars) + [VM] * len(operands) + [ANY] * len(deps),
        out_specs=[VM] * len(outs),
        out_shape=outs,
        scratch_shapes=list(scratch),
        compiler_params=params(32),
        cost_estimate=cost(flops, nbytes),
        name=name,
    )(*scalars, *operands, *deps)


def causal_mask():
    s = lax.broadcasted_iota(jnp.int32, (BLOCK, BLOCK), 0)
    u = lax.broadcasted_iota(jnp.int32, (BLOCK, BLOCK), 1)
    return s <= u


def adjoint_kernel(q_ref, g_ref, c_ref, out_ref):
    qt = (q_ref[...].astype(F32).T * c_ref[0:1, :]).astype(BF)
    out_ref[0, 0] = dot(qt, g_ref[...], 1, 0)


def tile_spec():
    return pl.BlockSpec(TILE, lambda i, h: (i, h))


def scale_spec():
    return pl.BlockSpec((8, BLOCK), lambda i, h: (0, i))


def state_spec():
    return pl.BlockSpec((1, 1, HD, HD), lambda i, h: (i, h, 0, 0))


def block_adjoints(queries, grads, scale):
    return pl.pallas_call(
        adjoint_kernel,
        grid=(2, LIN),
        in_specs=[tile_spec(), tile_spec(), scale_spec()],
        out_specs=state_spec(),
        out_shape=jax.ShapeDtypeStruct((2, LIN, HD, HD), F32),
        compiler_params=params(16),
        cost_estimate=cost(1e8, 2 * MIB),
        name="block_adjoints",
    )(queries, grads, scale)


def split(value):
    high = value.astype(BF)
    return high, (value - high.astype(F32)).astype(BF)


def linear_forward_kernel(q_ref, k_ref, v_ref, c_ref, s_ref, base_ref, out_ref):
    q, k, v, c = q_ref[...], k_ref[...], v_ref[...], c_ref[0:1, :]
    weights = jnp.where(causal_mask(), dot(k, q, 1, 1) * c, 0.0).astype(BF)
    hi, lo = split(s_ref[0, 0].T)
    out = dot(v, weights, 0, 0) + c * (dot(hi, q, 1, 1) + dot(lo, q, 1, 1))
    out_ref[...] = out.T.astype(BF)


def linear_forward(queries, keys, values, scale, before, base):
    return pl.pallas_call(
        linear_forward_kernel,
        grid=(2, LIN),
        in_specs=[tile_spec()] * 3 + [scale_spec(), state_spec(), ANY],
        out_specs=tile_spec(),
        out_shape=jax.ShapeDtypeStruct(queries.shape, BF),
        input_output_aliases={5: 0},
        compiler_params=params(12),
        cost_estimate=cost(2.4e9, 4 * MIB),
        name="linear_forward",
    )(queries, keys, values, scale, before, base)


def linear_backward_kernel(
    q_ref, k_ref, v_ref, g_ref, c_ref, s_ref, b0, b1, b2, dep, dq_ref, dk_ref, dv_ref
):
    q, k, v, g, c = q_ref[...], k_ref[...], v_ref[...], g_ref[...], c_ref[0:1, :]
    mask = causal_mask()
    grad_weights = jnp.where(mask, dot(v, g, 1, 1) * c, 0.0).astype(BF)
    hi, lo = split(s_ref[0, 0])
    dq = dot(k, grad_weights, 0, 0) + c * (dot(hi, g, 1, 1) + dot(lo, g, 1, 1))
    dq_ref[...] = dq.T.astype(BF)
    dk_ref[...] = dot(grad_weights, q, 1, 0)
    weights = jnp.where(mask, dot(k, q, 1, 1) * c, 0.0).astype(BF)
    dv_ref[...] = dot(weights, g, 1, 0)


def linear_backward(queries, keys, values, grads, scale, before, bases, dep):
    shape = queries.shape
    return pl.pallas_call(
        linear_backward_kernel,
        grid=(2, LIN),
        in_specs=[tile_spec()] * 4 + [scale_spec(), state_spec()] + [ANY] * 4,
        out_specs=[tile_spec()] * 3,
        out_shape=[jax.ShapeDtypeStruct(shape, t) for t in (BF, F32, F32)],
        input_output_aliases={6: 0, 7: 1, 8: 2},
        compiler_params=params(16),
        cost_estimate=cost(5e9, 9 * MIB),
        name="linear_backward",
    )(queries, keys, values, grads, scale, before, *bases, dep)


PIECES = 16


def sparse_forward_kernel(table, q_ref, k_ref, v_ref, *rest):
    pieces = rest[:PIECES]
    out_ref, kf_ref, vf_ref, log_ref, s_ref, sems = rest[PIECES:]
    step = pl.program_id(0)

    @pl.when(step == 0)
    def _():
        @pl.loop(0, 2 * LISTED)
        def _(row):
            for j in range(PIECES):
                for n, far in ((0, kf_ref), (1, vf_ref)):

                    @pl.when(table[row, 2 * n] == j)
                    def _():
                        at = pl.ds(pl.multiple_of(table[row, 2 * n + 1] * HD, HD), BLOCK)
                        pltpu.make_async_copy(pieces[j].at[at], far.at[row], sems.at[n, row]).start()

    q = q_ref[...]
    s = jnp.where(causal_mask(), dot(k_ref[...], q, 1, 1) * SCALING, -1e30)
    s_ref[0] = s
    peak = jnp.max(s, axis=0, keepdims=True)
    for r in range(LISTED):
        row = step * LISTED + r
        pltpu.make_async_copy(pieces[0].at[pl.ds(0, BLOCK)], kf_ref.at[row], sems.at[0, row]).wait()
        bias = jnp.where(table[row, 4] == 1, 0.0, -1e30).astype(F32)
        s = dot(kf_ref[row], q, 1, 1) * SCALING + bias
        s_ref[r + 1] = s
        peak = jnp.maximum(peak, jnp.max(s, axis=0, keepdims=True))
    total = jnp.zeros((1, BLOCK), F32)
    out = jnp.zeros((HD, BLOCK), F32)
    for r in range(LISTED + 1):
        e = jnp.exp(s_ref[r] - peak)
        total = total + jnp.sum(e, axis=0, keepdims=True)
        p = e.astype(BF)
        if r == 0:
            value = v_ref[...]
        else:
            row = step * LISTED + r - 1
            pltpu.make_async_copy(pieces[0].at[pl.ds(0, BLOCK)], vf_ref.at[row], sems.at[1, row]).wait()
            value = vf_ref[row]
        out = out + dot(value, p, 0, 0)
    log_ref[...] = jnp.broadcast_to(peak + jnp.log(total), (8, BLOCK))
    out_ref[...] = (out / total).T.astype(BF)


def sparse_forward(table, queries, keys, values, pieces):
    column = pl.BlockSpec(TILE, lambda i, t: (i, LIN))
    far = (2 * LISTED, BLOCK, HD)
    return pl.pallas_call(
        sparse_forward_kernel,
        grid_spec=pltpu.PrefetchScalarGridSpec(
            num_scalar_prefetch=1,
            grid=(2,),
            in_specs=[column] * 3 + [ANY] * PIECES,
            out_specs=[
                column,
                pl.BlockSpec(far, lambda i, t: (0, 0, 0)),
                pl.BlockSpec(far, lambda i, t: (0, 0, 0)),
                pl.BlockSpec((8, BLOCK), lambda i, t: (0, i)),
            ],
            scratch_shapes=[
                pltpu.VMEM((LISTED + 1, BLOCK, BLOCK), F32),
                pltpu.SemaphoreType.DMA((2, 2 * LISTED)),
            ],
        ),
        out_shape=[
            jax.ShapeDtypeStruct(queries.shape, BF),
            pltpu.HBM(far, BF),
            pltpu.HBM(far, BF),
            jax.ShapeDtypeStruct((8, queries.shape[0]), F32),
        ],
        compiler_params=params(20),
        cost_estimate=cost(4e9, 12 * MIB),
        name="sparse_forward",
    )(table, queries, keys, values, *pieces)


def sparse_backward_kernel(
    core, table, q_ref, k_ref, v_ref, g_ref, o_ref, kf_ref, vf_ref, log_ref, dq_ref, dk_ref, dv_ref, mine_ref, sent_ref
):
    first = core[0] == 0
    q, g = q_ref[...], g_ref[...]
    row_dot = jnp.sum((g.astype(F32) * o_ref[...].astype(F32)).T, axis=0, keepdims=True)
    logs = log_ref[0:1, :]
    dq = jnp.zeros((HD, BLOCK), F32)
    for r in range(LISTED + 1):
        key = k_ref[...] if r == 0 else kf_ref[r - 1]
        value = v_ref[...] if r == 0 else vf_ref[r - 1]
        s = dot(key, q, 1, 1) * SCALING
        if r == 0:
            p = jnp.exp(jnp.where(causal_mask(), s - logs, -1e30))
        else:
            used = table[pl.program_id(0) * LISTED + r - 1, 4] == 1
            p = jnp.exp(s - jnp.where(used, logs, 1e30))
        ds = (p * (dot(value, g, 1, 1) - row_dot)).astype(BF)
        dq = dq + dot(key, ds, 0, 0)
        dk = dot(ds, q, 1, 0) * SCALING
        dv = dot(p.astype(BF), g, 1, 0)
        if r == 0:
            dk_ref[...] = dk
            dv_ref[...] = dv
        else:
            mine_ref[r - 1] = jnp.where(first, dk, dv).astype(BF)
            sent_ref[r - 1] = jnp.where(first, dv, dk).astype(BF)
    dq_ref[...] = (dq * SCALING).T.astype(BF)


def sparse_backward(core, table, queries, keys, values, grads, outs, far_k, far_v, logs):
    column = pl.BlockSpec(TILE, lambda i, c, t: (i, LIN))
    four = pl.BlockSpec((LISTED, BLOCK, HD), lambda i, c, t: (i, 0, 0))
    return pl.pallas_call(
        sparse_backward_kernel,
        grid_spec=pltpu.PrefetchScalarGridSpec(
            num_scalar_prefetch=2,
            grid=(2,),
            in_specs=[column] * 3
            + [pl.BlockSpec(TILE, lambda i, c, t: (i, 0)), column, four, four]
            + [pl.BlockSpec((8, BLOCK), lambda i, c, t: (0, i))],
            out_specs=[column, column, column, four, four],
        ),
        out_shape=[
            jax.ShapeDtypeStruct(queries.shape, BF),
            jax.ShapeDtypeStruct(queries.shape, F32),
            jax.ShapeDtypeStruct(queries.shape, F32),
            jax.ShapeDtypeStruct((2 * LISTED, BLOCK, HD), BF),
            jax.ShapeDtypeStruct((2 * LISTED, BLOCK, HD), BF),
        ],
        compiler_params=params(20),
        cost_estimate=cost(8e9, 8 * MIB),
        name="sparse_backward",
    )(core, table, queries, keys, values, grads, outs, far_k, far_v, logs)


def begin_kernel(core, k_ref, v_ref, states, mine, sent):
    first = core[0] == 0
    for h in range(LIN):
        at = pl.ds(h * HD, HD)
        s0 = dot(k_ref[0:BLOCK, at], v_ref[0:BLOCK, at], 0, 0)
        s1 = dot(k_ref[BLOCK:, at], v_ref[BLOCK:, at], 0, 0)
        states[0, h] = s0
        states[1, h] = s1
        sent[2 * BLOCK + h * HD : 2 * BLOCK + (h + 1) * HD] = (s0 + s1).astype(BF)
    at = pl.ds(LIN * HD, HD)
    k, v = k_ref[:, at], v_ref[:, at]
    mine[...] = jnp.where(first, k, v)
    sent[0 : 2 * BLOCK] = jnp.where(first, v, k)


def start_kernel(core, mine, got, states, out, rest, scratch):
    out[0 : 2 * BLOCK] = mine[...]
    rest[...] = got[0 : 2 * BLOCK]
    for h in range(LIN):
        other = got[2 * BLOCK + h * HD : 2 * BLOCK + (h + 1) * HD].astype(F32)
        scratch[h * HD : (h + 1) * HD] = states[0, h] + states[1, h] + other
    out[2 * BLOCK : FRONT] = scratch[pl.ds(pl.multiple_of(core[0] * HALF, HALF), HALF)].astype(BF)


def line_kernel(core, earlier, sa, sb, ra, rb, fa, fb, la, lb, low, line, local):
    for n, (one, two) in enumerate(((sa, fa), (sb, fb), (ra, la), (rb, lb))):
        low[2 * BLOCK * n : 2 * BLOCK * (n + 1)] = one[0 : 2 * BLOCK]
        line[2 * BLOCK * n : 2 * BLOCK * (n + 1)] = two[0 : 2 * BLOCK]
    first = core[0] == 0
    s = [p[2 * BLOCK : FRONT].astype(F32) for p in (sa, ra, fa, la)]
    m = [earlier[0, p].astype(F32) for p in range(SIDE)]
    before = s[1] * m[1] + s[2] * m[2] + s[3] * m[3]
    total = s[0] + s[1] + s[2] + s[3]
    line[MID : MID + HALF] = jnp.where(first, total, s[0]).astype(BF)
    line[MID + HALF : MID + 2 * HALF] = jnp.where(first, 0.0, before).astype(BF)
    local[...] = before


def prefix_kernel(earlier, local, right, far, left, *rest):
    out, scratch, sems = rest[-3:]
    got = [
        pltpu.make_async_copy(piece.at[pl.ds(MID, 2 * HALF)], scratch.at[n], sems.at[n])
        for n, piece in enumerate((right, far, left))
    ]
    for copy in got:
        copy.start()
    for copy in got:
        copy.wait()
    total = local[...]
    for n in range(3):
        total = total + scratch[n, 0:HALF].astype(F32) * earlier[1, n + 1].astype(F32)
        total = total + scratch[n, HALF:].astype(F32)
    out[...] = total


def prefix(earlier, local, right, far, left, deps):
    return pl.pallas_call(
        prefix_kernel,
        in_specs=[SM, VM] + [ANY] * (3 + len(deps)),
        out_specs=VM,
        out_shape=jax.ShapeDtypeStruct((HALF, HD), F32),
        scratch_shapes=[pltpu.VMEM((3, 2 * HALF, HD), BF), pltpu.SemaphoreType.DMA((3,))],
        compiler_params=params(4),
        cost_estimate=cost(1e5, MIB // 2),
        name="prefix",
    )(earlier, local, right, far, left, *deps)


SPOTS = (0, BLOCK, FRONT, FRONT + BLOCK)


def placed(table, j, own_ref, peer_ref):
    a, b = table[0, j], table[1, j]
    first = own_ref[jnp.maximum(a, 0)].astype(F32) * jnp.where(a >= 0, 1.0, 0.0).astype(F32)
    second = peer_ref[jnp.maximum(b, 0)].astype(F32) * jnp.where(b >= 0, 1.0, 0.0).astype(F32)
    return first + second


def fill(table, own, peer, half, j, out, u, more=(), m=0):
    for q, spot in enumerate(SPOTS):
        at = pl.ds(spot, BLOCK)
        value = placed(table, 4 * j + q, own, peer)
        for ref in more:
            value = value + ref[m, at].astype(F32)
        out[u, at] = value.astype(BF)
    at = pl.ds(2 * BLOCK, HALF)
    value = half[...] * table[2, j].astype(F32)
    for ref in more:
        value = value + ref[m, at].astype(F32)
    out[u, at] = value.astype(BF)


def far_kernel(table, own, peer, half, far_a, far_b):
    @pl.loop(0, 2)
    def _(u):
        fill(table, own, peer, half, 8 + u, far_a, u)
        fill(table, own, peer, half, 10 + u, far_b, u)


def free_kernel(table, own, peer, half, right, left):
    @pl.loop(0, 2)
    def _(u):
        fill(table, own, peer, half, 6 + u, right, u)
        fill(table, own, peer, half, 12 + u, left, u)


def near_kernel(table, own, peer, half, ra, rb, right, left):
    @pl.loop(0, 2)
    def _(u):
        fill(table, own, peer, half, 4 + u, right, u, [ra], u)
        fill(table, own, peer, half, 14 + u, left, u, [rb], u)


def turn_kernel(table, own, peer, half, rl, rh, ll, lh, home, right_a, right_b, far_a, far_b, left_a, left_b, unit):
    @pl.loop(0, 2)
    def _(u):
        fill(table, own, peer, half, u, unit, u, [rl, ll], u)
        fill(table, own, peer, half, 2 + u, unit, 2 + u, [rh, lh], u)

    home[...] = unit[0]
    for n, (a, b) in ((1, (right_a, right_b)), (2, (far_a, far_b)), (3, (left_a, left_b))):
        a[...] = unit[n, 0:FRONT]
        b[...] = unit[n, FRONT:]


def last_kernel(right, left, ra, rb, o_right, o_left):
    o_right[...] = (right[...].astype(F32) + ra[...].astype(F32)).astype(BF)
    o_left[...] = (left[...].astype(F32) + rb[...].astype(F32)).astype(BF)


def tail_kernel(home, ra, rb, la, lb, mine, sent, extra):
    front = home[0:FRONT].astype(F32) + ra[...].astype(F32) + la[...].astype(F32)
    mine[...] = front[0 : 2 * BLOCK].astype(BF)
    extra[...] = front[2 * BLOCK :]
    sent[2 * BLOCK :] = front[2 * BLOCK :].astype(BF)
    back = home[FRONT:].astype(F32) + rb[...].astype(F32) + lb[...].astype(F32)
    sent[0 : 2 * BLOCK] = back.astype(BF)


def finish_kernel(core, k_ref, v_ref, dk, dv, mine_ref, got_ref, tail_ref, extra, adj, peer, kg, vg, scratch):
    first = core[0] == 0
    mine, got = mine_ref[...].astype(F32), got_ref[...].astype(F32)
    at = pl.ds(LIN * HD, HD)
    kg[:, at] = (dk[:, at] + jnp.where(first, mine, got)).astype(BF)
    vg[:, at] = (dv[:, at] + jnp.where(first, got, mine)).astype(BF)
    tail = tail_ref[...].astype(F32)
    scratch[0:HALF] = jnp.where(first, extra[...], tail)
    scratch[HALF:] = jnp.where(first, tail, extra[...])
    inner = jnp.where(pl.program_id(0) == 0, 1.0, 0.0).astype(F32)
    chip = jnp.where(first, 1.0, 0.0).astype(F32)
    for h in range(LIN):
        at = pl.ds(h * HD, HD)
        state = scratch[at, :] + peer[at, :].astype(F32) * chip + adj[1, h] * inner
        hi, lo = split(state)
        k, v = k_ref[:, at], v_ref[:, at]
        kg[:, at] = (dk[:, at] + dot(v, hi, 1, 1) + dot(v, lo, 1, 1)).astype(BF)
        vg[:, at] = (dv[:, at] + dot(k, hi, 1, 0) + dot(k, lo, 1, 0)).astype(BF)


def finish(core, keys, values, dk, dv, mine, got, extra, adjoints, peer):
    rows = pl.BlockSpec((BLOCK, keys.shape[1]), lambda i, c: (i, 0))
    piece = pl.BlockSpec((BLOCK, HD), lambda i, c: (i, 0))
    fixed = [
        pl.BlockSpec((HALF, HD), lambda i, c: (0, 0)),
        pl.BlockSpec(adjoints.shape, lambda i, c: (0, 0, 0, 0)),
        pl.BlockSpec((LIN * HD, HD), lambda i, c: (0, 0)),
    ]
    shape = jax.ShapeDtypeStruct(keys.shape, BF)
    return pl.pallas_call(
        finish_kernel,
        grid_spec=pltpu.PrefetchScalarGridSpec(
            num_scalar_prefetch=1,
            grid=(2,),
            in_specs=[rows] * 4 + [piece, piece, fixed[0]] + fixed,
            out_specs=[rows, rows],
            scratch_shapes=[pltpu.VMEM((LIN * HD, HD), F32)],
        ),
        out_shape=[shape, shape],
        compiler_params=params(32),
        cost_estimate=cost(5e8, 9 * MIB),
        name="finish",
    )(core, keys, values, dk, dv, mine, got, got[2 * BLOCK :], extra, adjoints, peer)


def where_is(blocks, place):
    owner, within = blocks // 2, blocks % 2
    pz = (place // (SIDE * CORES) - owner // (SIDE * CORES)) % SIDE
    px = (place // CORES % SIDE - owner // CORES % SIDE) % SIDE
    return pz, px, owner % CORES, within


def spot_of(blocks, place, stream):
    pz, px, core, within = where_is(blocks, place)
    rel = (core != stream).astype(jnp.int32)
    outer = jnp.where(stream == 0, pz, px)
    first = jnp.where(stream == 0, px, pz)
    return outer, first, rel * 2 + within


def spot_of(blocks, place, stream):
    pz, px, core, within = where_is(blocks, place)
    rel = (core != stream).astype(jnp.int32)
    outer = jnp.where(stream == 0, pz, px)
    first = jnp.where(stream == 0, px, pz)
    return outer, first, rel * 2 + within


def piece_of(blocks, place, stream):
    outer, first, rest = spot_of(blocks, place, stream)
    index = first % 2 * 16 + rest * 4
    return outer * 2 + first // 2 + 8 * (place % CORES != stream).astype(jnp.int32), index


def fetch_table(lists, place):
    flat = lists.reshape(-1)
    mine = place * 2 + jnp.arange(2 * LISTED, dtype=jnp.int32) // LISTED
    usable = (flat != mine).astype(jnp.int32)
    columns = [*piece_of(flat, place, 0), *piece_of(flat, place, 1), usable]
    return jnp.stack(columns, axis=1).astype(jnp.int32)


def back_table(lists, peer_lists, place):
    slots = jnp.arange(2 * LISTED, dtype=jnp.int32)[:, None]
    spots = jnp.arange(64, dtype=jnp.int32)[None, :]
    rows = []
    for some in (lists, peer_lists):
        outer, first, rest = spot_of(some.reshape(-1), place, place % CORES)
        target = (-outer) % SIDE * 16 + (-first) % SIDE * 4 + rest
        rows.append(jnp.max(jnp.where(target[:, None] == spots, slots, -1), axis=0))
    z, x = place // (SIDE * CORES), place // CORES % SIDE
    step = jnp.arange(64, dtype=jnp.int32)
    outer, inner = step // SIDE, step % SIDE
    on_keys = place % CORES == 0
    to_z = (z + jnp.where(on_keys, outer, inner)) % SIDE
    to_x = (x + jnp.where(on_keys, inner, outer)) % SIDE
    rows.append((to_z * SIDE + to_x < z * SIDE + x).astype(jnp.int32))
    return jnp.stack(rows).astype(jnp.int32)


def earlier_table(place):
    z, x = place // (SIDE * CORES), place // CORES % SIDE
    on_keys = place % CORES == 0
    first, second = jnp.where(on_keys, x, z), jnp.where(on_keys, z, x)
    step = jnp.arange(SIDE, dtype=jnp.int32)
    rows = [(c - step) % SIDE < c for c in (first, second)]
    return jnp.stack(rows).astype(jnp.int32)


def local(queries, keys, values, out_weight, out_grad, long_blocks):
    place = lax.axis_index("ctx").astype(jnp.int32)
    core = (place % CORES).reshape(1)
    row_count = queries.shape[0]
    positions = place * row_count + jnp.arange(row_count, dtype=jnp.int32)
    scale = 1.0 / (math.sqrt(HD) * jnp.sqrt((positions + 1).astype(F32)))
    scale = jnp.broadcast_to(scale[None, :], (8, row_count))
    lists = lax.dynamic_slice_in_dim(long_blocks, place * 2, 2, 0)
    peer_lists = lax.dynamic_slice_in_dim(long_blocks, (place ^ 1) * 2, 2, 0)
    fetch = fetch_table(lists, place)
    back = back_table(lists, peer_lists, place)
    earlier = earlier_table(place)

    grad_all = lax.all_gather(out_grad, "head", axis=1, tiled=True)

    states, mine, sent = whole_call(
        begin_kernel,
        [core],
        [keys, values],
        [((2, LIN, HD, HD), F32), ((2 * BLOCK, HD), BF), ((2 * BLOCK + LIN * HD, HD), BF)],
        "begin",
    )
    got = swap(sent)
    sa, sb = whole_call(
        start_kernel, [core], [mine, got, states], [((FRONT, HD), BF), ((2 * BLOCK, HD), BF)], "start",
        scratch=[pltpu.VMEM((LIN * HD, HD), F32)],
    )
    ra, lb = ring_move(sa, 0, 1), ring_move(sb, 0, -1)
    rb, la = ring_move(sb, 0, 1), ring_move(sa, 0, -1)
    fa, fb = ring_move(ra, 0, 1), ring_move(lb, 0, -1)
    low, high, inside = whole_call(
        line_kernel, [core, earlier], [sa, sb, ra, rb, fa, fb, la, lb],
        [((MID, HD), BF), ((MID + 2 * HALF, HD), BF), ((HALF, HD), F32)], "line",
    )
    low_right, low_left = ring_move(low, 1, 1), ring_move(low, 1, -1)
    high_left, high_right = ring_move(high, 1, -1), ring_move(high, 1, 1)
    low_far, high_far = ring_move(low_right, 1, 1), ring_move(high_left, 1, -1)
    pieces = [low, high, low_right, high_right, low_far, high_far, low_left, high_left]
    swapped = [swap(p) for p in pieces]
    pieces = pieces + swapped
    done = [low_far, low_left, *swapped[:4], *swapped[6:]]
    part = prefix(earlier, inside, high_right, high_far, high_left, done)
    other = swap(part)
    on_keys = place % CORES == 0
    chip = jnp.where(on_keys, jnp.concatenate([part, other]), jnp.concatenate([other, part]))
    chip = chip + jnp.where(on_keys, 0.0, got[2 * BLOCK :].astype(F32))
    chip = chip.reshape(LIN, HD, HD)
    before = jnp.stack([chip, chip + states[0]])

    sparse_out, far_k, far_v, logs = sparse_forward(fetch, queries, keys, values, pieces)
    attention = linear_forward(queries, keys, values, scale, before, sparse_out)
    partial_out = dot(attention, out_weight, 1, 1).astype(BF)
    layer_out = lax.psum_scatter(partial_out, "head", scatter_dimension=1, tiled=True)
    sparse_grad = dot(grad_all, out_weight[:, LIN * HD :], 1, 0).astype(BF)
    linear_grad = dot(grad_all, out_weight[:, : LIN * HD], 1, 0).astype(BF)
    query_grad, own_dk, own_dv, pair_mine, pair_sent = sparse_backward(
        core, fetch, queries, keys, values, sparse_grad, attention, far_k, far_v, logs
    )

    adjoints = block_adjoints(queries, linear_grad, scale)
    adjoint = (adjoints[0] + adjoints[1]).reshape(LIN * HD, HD)
    adjoint_peer = swap(adjoint.astype(BF))
    half = lax.dynamic_slice_in_dim(
        adjoint + adjoint_peer.astype(F32), place % CORES * HALF, HALF, 0
    )
    base = [pair_mine, swap(pair_sent), half]
    far_a, far_b = whole_call(
        far_kernel, [back], base, [((2, UNIT, HD), BF)] * 2, "back_far"
    )
    ra, rb = ring_move(far_a, 1, 1), ring_move(far_b, 1, -1)
    pair = [((2, UNIT, HD), BF)] * 2
    free = whole_call(free_kernel, [back], base, pair, "back_free", deps=[far_a])
    rh, ll = ring_move(free[0], 1, 1), ring_move(free[1], 1, -1)
    near = whole_call(near_kernel, [back], base + [ra, rb], pair, "back_near")
    rl, lh = ring_move(near[0], 1, 1), ring_move(near[1], 1, -1)
    query_grad, own_dk, own_dv = linear_backward(
        queries, keys, values, linear_grad, scale, before, (query_grad, own_dk, own_dv), inside
    )

    front, rear = ((FRONT, HD), BF), ((2 * BLOCK, HD), BF)
    home, right_a, right_b, far_a, far_b, left_a, left_b = whole_call(
        turn_kernel, [back], base + [rl, rh, ll, lh], [((UNIT, HD), BF)] + [front, rear] * 3,
        "back_turn", deps=[query_grad], scratch=[pltpu.VMEM((SIDE, UNIT, HD), BF)],
    )
    ra, rb = ring_move(far_a, 0, 1), ring_move(far_b, 0, -1)
    to_rb, to_la = ring_move(right_b, 0, 1), ring_move(left_a, 0, -1)
    right_a, left_b = whole_call(last_kernel, [], [right_a, left_b, ra, rb], [front, rear], "back_last")
    to_ra, to_lb = ring_move(right_a, 0, 1), ring_move(left_b, 0, -1)
    mine, sent, extra = whole_call(
        tail_kernel, [], [home, to_ra, to_rb, to_la, to_lb],
        [rear, front, ((HALF, HD), F32)], "back_tail",
    )
    key_grad, value_grad = finish(
        core, keys, values, own_dk, own_dv, mine, swap(sent), extra, adjoints, adjoint_peer
    )
    return layer_out, query_grad, key_grad, value_grad


def solution(mesh):
    return jax.shard_map(
        local,
        mesh=mesh,
        in_specs=(
            P("ctx", "head"),
            P("ctx", "head"),
            P("ctx", "head"),
            P(None, "head"),
            P("ctx", "head"),
            P(),
        ),
        out_specs=(P("ctx", "head"), P("ctx", "head"), P("ctx", "head"), P("ctx", "head")),
        check_vma=False,
    )
```
